32 devices in a mesh: dp: 16 (over z, y, x), tensor: 2 (over core).
Axes of the slice: x: 2, y: 2, z: 4, core: 2. Of those that a mesh axis runs over, the one named last changes fastest.
Arguments:
- tokens: bfloat16 [4096, 1024], P(('dp', 'tensor')), may hold values from -6 to 6
- cotangent: bfloat16 [4096, 1024], P(('dp', 'tensor')), may hold values from -6 to 6
- lengths: int32 [16], P('dp'), may hold values from 64 to 256, as said below
- w_query: bfloat16 [1024, 2048], P('dp', 'tensor'), may hold values from -0.1875 to 0.1875
- key_matrix: bfloat16 [1024, 1024], P('dp', 'tensor'), may hold values from -0.1875 to 0.1875
- value_matrix: bfloat16 [1024, 1024], P('dp', 'tensor'), may hold values from -0.1875 to 0.1875
- w_out: bfloat16 [1024, 2048], P('dp', 'tensor'), may hold values from -0.375 to 0.375
- w_gate: bfloat16 [1024, 3072], P('dp', 'tensor'), may hold values from -0.1875 to 0.1875
- w_up: bfloat16 [1024, 3072], P('dp', 'tensor'), may hold values from -0.1875 to 0.1875
- w_down: bfloat16 [1024, 3072], P('dp', 'tensor'), may hold values from -0.109375 to 0.109375
- gain_attn: float32 [1024], replicated, may hold values from 0.5 to 2
- gain_mlp: float32 [1024], replicated, may hold values from 0.5 to 2
- gain_query: float32 [128], replicated, may hold values from 0.5 to 2
- gain_key: float32 [128], replicated, may hold values from 0.5 to 2
Outputs:
- result: bfloat16 [4096, 1024], P(('dp', 'tensor'))
- grad_tokens: float32 [4096, 1024], P(('dp', 'tensor'))
- grad_w_query: float32 [1024, 2048], P('dp', 'tensor')
- grad_w_key: float32 [1024, 1024], P('dp', 'tensor')
- grad_w_value: float32 [1024, 1024], P('dp', 'tensor')
- grad_w_out: float32 [1024, 2048], P('dp', 'tensor')
- grad_w_gate: float32 [1024, 3072], P('dp', 'tensor')
- grad_w_up: float32 [1024, 3072], P('dp', 'tensor')
- grad_w_down: float32 [1024, 3072], P('dp', 'tensor')
- grad_gain_attn: float32 [1024], replicated
- grad_gain_mlp: float32 [1024], replicated
- grad_gain_query: float32 [128], replicated
- grad_gain_key: float32 [128], replicated
The draws below stay inside these ranges and needn't reach their ends.
Inputs may be any that keep to these rules, and one draw needn't show every extreme that they name: `lengths`: some sequence fills all 256 token slots of its block.
All inputs are finite; a program needn't handle non-finite values.
Results may differ from the reference program's by a relative error of at most 0.013.
The reference program's roundings to bfloat16 on the way count: a program that leaves them out, or rounds other values in their place, can miss the bound.
Values may be sent and summed in bfloat16 or wider, within the bound.
A program may use at most 128 MiB of HBM per device.

```python
import math
import jax
import jax.numpy as jnp
from jax import lax

MODEL_WIDTH = 1024
QUERY_HEADS = 16
KEY_VALUE_HEADS = 8
HEAD_SIZE = 128
FF = 3072
TOK_DP = 256
TOKENS = 4096
N_DP = 16


def draw_lengths(key, part):
    drawn = jax.random.randint(key, (N_DP,), TOK_DP // 4, TOK_DP + 1, dtype=jnp.int32)
    slots = jnp.arange(N_DP, dtype=jnp.int32)
    drawn = jnp.where(slots == 0, jnp.int32(TOK_DP), drawn)
    drawn = jnp.where(slots == N_DP - 1, jnp.int32(TOK_DP // 4), drawn)
    return drawn.astype(jnp.int32)


def block_levels(key, dims, cuts, smallest, high):
    loudness = 1.0
    for dim, shards_of in cuts:
        heights = jax.random.uniform(jax.random.fold_in(jax.random.fold_in(key, 6), dim), (shards_of,), jnp.float32, smallest / len(cuts), high / len(cuts))
        loudness = loudness * jnp.repeat(jnp.exp(heights), dims[dim] // shards_of).reshape((-1,) + (1,) * (len(dims) - 1 - dim))
    return loudness


def gaussian(key, shape, spread, limit, split=(), kind=jnp.bfloat16):
    array = spread * jax.random.normal(key, shape, jnp.float32)
    if split:
        array = array * block_levels(key, shape, split, -0.22, 0.18)
    return jnp.clip(array, -limit, limit).astype(kind)


def setup_inputs(seed: int = 0) -> dict:
    seeds = jax.random.split(jax.random.key(seed), 15)
    tokens = gaussian(seeds[0], (TOKENS, MODEL_WIDTH), 1.0, 6.0, ((0, 32),))
    cotangent = gaussian(seeds[1], (TOKENS, MODEL_WIDTH), 1.0, 6.0, ((0, 32),))
    lengths = draw_lengths(jax.random.fold_in(seeds[14], 71), 0)
    w_query = gaussian(seeds[3], (MODEL_WIDTH, QUERY_HEADS * HEAD_SIZE), MODEL_WIDTH ** -0.5, 0.1875, ((0, 16), (1, 2)))
    key_matrix = gaussian(seeds[4], (MODEL_WIDTH, KEY_VALUE_HEADS * HEAD_SIZE), MODEL_WIDTH ** -0.5, 0.1875, ((0, 16), (1, 2)))
    value_matrix = gaussian(seeds[5], (MODEL_WIDTH, KEY_VALUE_HEADS * HEAD_SIZE), MODEL_WIDTH ** -0.5, 0.1875, ((0, 16), (1, 2)))
    w_out = gaussian(seeds[6], (MODEL_WIDTH, QUERY_HEADS * HEAD_SIZE), (QUERY_HEADS * HEAD_SIZE // 8) ** -0.5, 0.375, ((0, 16), (1, 2)))
    w_gate = gaussian(seeds[7], (MODEL_WIDTH, FF), MODEL_WIDTH ** -0.5, 0.1875, ((0, 16), (1, 2)))
    w_up = gaussian(seeds[8], (MODEL_WIDTH, FF), MODEL_WIDTH ** -0.5, 0.1875, ((0, 16), (1, 2)))
    w_down = gaussian(seeds[9], (MODEL_WIDTH, FF), FF ** -0.5, 0.109375, ((0, 16), (1, 2)))
    gain_attn = jnp.clip(jnp.exp(jax.random.uniform(seeds[10], (MODEL_WIDTH,), jnp.float32, math.log(0.5), math.log(2.0))), 0.5, 2.0)
    gain_mlp = jnp.clip(jnp.exp(jax.random.uniform(seeds[11], (MODEL_WIDTH,), jnp.float32, math.log(0.5), math.log(2.0))), 0.5, 2.0)
    gain_query = jnp.clip(jnp.exp(jax.random.uniform(seeds[12], (HEAD_SIZE,), jnp.float32, math.log(0.5), math.log(2.0))), 0.5, 2.0)
    gain_key = jnp.clip(jnp.exp(jax.random.uniform(seeds[13], (HEAD_SIZE,), jnp.float32, math.log(0.5), math.log(2.0))), 0.5, 2.0)
    return {"tokens": tokens, "cotangent": cotangent, "lengths": lengths, "w_query": w_query, "key_matrix": key_matrix, "value_matrix": value_matrix, "w_out": w_out, "w_gate": w_gate, "w_up": w_up, "w_down": w_down, "gain_attn": gain_attn, "gain_mlp": gain_mlp, "gain_query": gain_query, "gain_key": gain_key}


norm_eps = 1e-06
rope_base = 1000000.0

def rms_rows(values, gain_vec):
    inverse = lax.rsqrt(lax.optimization_barrier(jnp.mean(values * values, axis=-1, keepdims=True)) + norm_eps)
    return (values * inverse * gain_vec, inverse)

def rms_back(grad_output, values, inverse, gain_vec):
    scaled = grad_output * gain_vec
    mean_term = lax.optimization_barrier(jnp.mean(scaled * values, axis=-1, keepdims=True))
    grad_values = inverse * scaled - values * (inverse * inverse * inverse) * mean_term
    flat_terms = (grad_output * values * inverse).reshape(-1, values.shape[-1])
    return (grad_values, lax.optimization_barrier(jnp.sum(flat_terms, axis=0)))

def layout(length_value, total_rows):
    length_value = jnp.asarray(length_value).astype(jnp.int32)
    indices = jnp.arange(total_rows, dtype=jnp.int32)
    live = indices < length_value
    positions = jnp.where(live, indices, jnp.zeros_like(indices)).astype(jnp.int32)
    causal = live[:, None] & live[None, :] & (indices[None, :] <= indices[:, None])
    allowed = causal | (indices[:, None] == indices[None, :])
    return (positions, allowed, live)

def rope_tables(positions, head_width):
    half_width = head_width // 2
    frequency = jnp.exp(-jnp.log(rope_base) * (2.0 * jnp.arange(half_width, dtype=jnp.float32) / head_width))
    angles = positions.astype(jnp.float32)[:, None] * frequency[None, :]
    return (jnp.cos(angles), jnp.sin(angles))

def rotate(values, cosine, sine_part):
    half_width = values.shape[-1] // 2
    first, second = (values[..., :half_width], values[..., half_width:])
    return jnp.concatenate([first * cosine - second * sine_part, second * cosine + first * sine_part], axis=-1)

def rotate_back(grads, cosine, sine_part):
    half_width = grads.shape[-1] // 2
    first, second = (grads[..., :half_width], grads[..., half_width:])
    return jnp.concatenate([first * cosine + second * sine_part, second * cosine - first * sine_part], axis=-1)

def masked_scores(query_rot, key_rot, allowed, scaling):
    scores = jnp.einsum('qgrd,kgd->grqk', query_rot.astype(jnp.float32), key_rot.astype(jnp.float32)) * scaling
    return jnp.where(allowed, scores, -1e+30)

def layer_group(tokens, cotangent, length_value, params):
    w_query, key_matrix, value_matrix, w_out, w_gate, w_up, w_down, gain_attn, gain_mlp, gain_query, gain_key = params
    total_rows = tokens.shape[0]
    kv_heads = key_matrix.shape[1] // HEAD_SIZE
    group_ratio = w_query.shape[1] // key_matrix.shape[1]
    scaling = HEAD_SIZE ** (-0.5)
    positions, allowed, live = layout(length_value, total_rows)
    cot_live = jnp.where(live[:, None], cotangent, jnp.zeros_like(cotangent))
    cosine, sine_part = rope_tables(positions, HEAD_SIZE)
    cos_query, sin_query = (cosine[:, None, None, :], sine_part[:, None, None, :])
    cos_key, sin_key = (cosine[:, None, :], sine_part[:, None, :])
    token_values = tokens.astype(jnp.float32)
    attn_norm, attn_inverse = rms_rows(token_values, gain_attn)
    normed = attn_norm.astype(jnp.bfloat16)
    query_raw = jnp.dot(normed, w_query, preferred_element_type=jnp.float32).reshape(total_rows, kv_heads, group_ratio, HEAD_SIZE)
    key_raw = jnp.dot(normed, key_matrix, preferred_element_type=jnp.float32).reshape(total_rows, kv_heads, HEAD_SIZE)
    value_part = jnp.dot(normed, value_matrix, preferred_element_type=jnp.float32).astype(jnp.bfloat16).reshape(total_rows, kv_heads, HEAD_SIZE)
    query_normed, query_inverse = rms_rows(query_raw, gain_query)
    key_normed, key_inverse = rms_rows(key_raw, gain_key)
    query_rot = rotate(query_normed, cos_query, sin_query).astype(jnp.bfloat16)
    key_rot = rotate(key_normed, cos_key, sin_key).astype(jnp.bfloat16)
    scores = masked_scores(query_rot, key_rot, allowed, scaling)
    row_max = lax.optimization_barrier(jnp.max(scores, axis=-1, keepdims=True))
    log_total = row_max + jnp.log(lax.optimization_barrier(jnp.sum(jnp.exp(scores - row_max), axis=-1, keepdims=True)))
    attn_probs = jnp.exp(scores - log_total).astype(jnp.bfloat16)
    mixed = jnp.einsum('grqk,kgd->qgrd', attn_probs.astype(jnp.float32), value_part.astype(jnp.float32)).astype(jnp.bfloat16)
    mixed_flat = mixed.reshape(total_rows, -1)
    resid = token_values + jnp.dot(mixed_flat, w_out.T, preferred_element_type=jnp.float32)
    mlp_norm, mlp_inverse = rms_rows(resid, gain_mlp)
    mlp_in = mlp_norm.astype(jnp.bfloat16)
    gate_proj = jnp.dot(mlp_in, w_gate, preferred_element_type=jnp.float32)
    up_proj = jnp.dot(mlp_in, w_up, preferred_element_type=jnp.float32)
    activation = (jax.nn.silu(gate_proj) * up_proj).astype(jnp.bfloat16)
    result = (resid + jnp.dot(activation, w_down.T, preferred_element_type=jnp.float32)).astype(jnp.bfloat16)
    grad_w_down = jnp.dot(cot_live.T, activation, preferred_element_type=jnp.float32)
    grad_act = jnp.dot(cot_live, w_down, preferred_element_type=jnp.float32)
    sigma = jax.nn.sigmoid(gate_proj)
    grad_gate = (grad_act * up_proj * sigma * (1.0 + gate_proj * (1.0 - sigma))).astype(jnp.bfloat16)
    grad_up = (grad_act * gate_proj * sigma).astype(jnp.bfloat16)
    grad_w_gate = jnp.dot(mlp_in.T, grad_gate, preferred_element_type=jnp.float32)
    grad_w_up = jnp.dot(mlp_in.T, grad_up, preferred_element_type=jnp.float32)
    grad_mlp_in = jnp.dot(grad_gate, w_gate.T, preferred_element_type=jnp.float32) + jnp.dot(grad_up, w_up.T, preferred_element_type=jnp.float32)
    grad_resid_mlp, grad_gain_mlp = rms_back(grad_mlp_in, resid, mlp_inverse, gain_mlp)
    grad_resid = cot_live.astype(jnp.float32) + grad_resid_mlp
    grad_attn = grad_resid.astype(jnp.bfloat16)
    grad_w_out = jnp.dot(grad_attn.T, mixed_flat, preferred_element_type=jnp.float32)
    grad_mixed = jnp.dot(grad_attn, w_out, preferred_element_type=jnp.float32).astype(jnp.bfloat16).reshape(total_rows, kv_heads, group_ratio, HEAD_SIZE)
    scores = masked_scores(query_rot, key_rot, allowed, scaling)
    probs_full = jnp.exp(scores - log_total)
    probs_half = probs_full.astype(jnp.bfloat16)
    grad_value = jnp.einsum('grqk,qgrd->kgd', probs_half.astype(jnp.float32), grad_mixed.astype(jnp.float32))
    grad_probs = jnp.einsum('qgrd,kgd->grqk', grad_mixed.astype(jnp.float32), value_part.astype(jnp.float32))
    row_delta = lax.optimization_barrier(jnp.sum(grad_mixed.astype(jnp.float32) * mixed.astype(jnp.float32), axis=-1))
    row_delta = jnp.transpose(row_delta, (1, 2, 0))[..., None]
    grad_scores = (probs_full * (grad_probs - row_delta) * scaling).astype(jnp.bfloat16)
    grad_query_rot = jnp.einsum('grqk,kgd->qgrd', grad_scores.astype(jnp.float32), key_rot.astype(jnp.float32))
    grad_key_rot = jnp.einsum('grqk,qgrd->kgd', grad_scores.astype(jnp.float32), query_rot.astype(jnp.float32))
    grad_query_raw, grad_gain_query = rms_back(rotate_back(grad_query_rot, cos_query, sin_query), query_raw, query_inverse, gain_query)
    grad_key_raw, grad_gain_key = rms_back(rotate_back(grad_key_rot, cos_key, sin_key), key_raw, key_inverse, gain_key)
    grad_query_half = grad_query_raw.astype(jnp.bfloat16).reshape(total_rows, -1)
    grad_key_half = grad_key_raw.astype(jnp.bfloat16).reshape(total_rows, -1)
    grad_value_half = grad_value.astype(jnp.bfloat16).reshape(total_rows, -1)
    grad_w_query = jnp.dot(normed.T, grad_query_half, preferred_element_type=jnp.float32)
    grad_w_key = jnp.dot(normed.T, grad_key_half, preferred_element_type=jnp.float32)
    grad_w_value = jnp.dot(normed.T, grad_value_half, preferred_element_type=jnp.float32)
    grad_normed = jnp.dot(grad_query_half, w_query.T, preferred_element_type=jnp.float32)
    grad_normed = grad_normed + jnp.dot(grad_key_half, key_matrix.T, preferred_element_type=jnp.float32)
    grad_normed = grad_normed + jnp.dot(grad_value_half, value_matrix.T, preferred_element_type=jnp.float32)
    grad_tokens_attn, grad_gain_attn = rms_back(grad_normed, token_values, attn_inverse, gain_attn)
    grad_tokens = grad_resid + grad_tokens_attn
    grads = (grad_w_query, grad_w_key, grad_w_value, grad_w_out, grad_w_gate, grad_w_up, grad_w_down, grad_gain_attn, grad_gain_mlp, grad_gain_query, grad_gain_key)
    return (result, grad_tokens, grads)

def reference(tokens, cotangent, lengths, w_query, key_matrix, value_matrix, w_out, w_gate, w_up, w_down, gain_attn, gain_mlp, gain_query, gain_key):
    params = (w_query, key_matrix, value_matrix, w_out, w_gate, w_up, w_down, gain_attn, gain_mlp, gain_query, gain_key)
    packs = tokens.reshape(N_DP, TOK_DP, MODEL_WIDTH)
    pack_grads = cotangent.reshape(N_DP, TOK_DP, MODEL_WIDTH)
    initial = tuple((jnp.zeros(item.shape, jnp.float32) for item in params))

    def one_pack(carry, item):
        pack_tokens, pack_cotangent, length_value = item
        result, grad_tokens, grads = layer_group(pack_tokens, pack_cotangent, length_value, params)
        summed = tuple((left + right for left, right in zip(carry, grads)))
        return (summed, (result, grad_tokens))
    totals, (results, grad_rows) = lax.scan(one_pack, initial, (packs, pack_grads, lengths.astype(jnp.int32)))
    return (results.reshape(TOKENS, MODEL_WIDTH), grad_rows.reshape(TOKENS, MODEL_WIDTH), totals[0], totals[1], totals[2], totals[3], totals[4], totals[5], totals[6], totals[7], totals[8], totals[9], totals[10])
```

```python
import functools
import math

import jax
import jax.numpy as jnp
from jax import lax
from jax.experimental import pallas as pl
from jax.experimental.pallas import tpu as pltpu
from jax.sharding import PartitionSpec as P

MESH = pl.DeviceIdType.MESH
VMEM_LIMIT = 64000000

QUERY_HEADS = 16
KEY_VALUE_HEADS = 8
HEAD_SIZE = 128


norm_eps = 1e-06
rope_base = 1000000.0


def rms_rows(values, gain_vec):
    inverse = lax.rsqrt(jnp.mean(values * values, axis=-1, keepdims=True) + norm_eps)
    return (values * inverse * gain_vec, inverse)


def rms_back(grad_output, values, inverse, gain_vec):
    scaled = grad_output * gain_vec
    mean_term = jnp.mean(scaled * values, axis=-1, keepdims=True)
    grad_values = inverse * scaled - values * (inverse * inverse * inverse) * mean_term
    flat_terms = (grad_output * values * inverse).reshape(-1, values.shape[-1])
    return (grad_values, jnp.sum(flat_terms, axis=0))


def layout(length_value, total_rows):
    length_value = jnp.asarray(length_value)
    indices = jnp.arange(total_rows, dtype=jnp.int32)
    live = indices < length_value
    positions = jnp.where(live, indices, jnp.zeros_like(indices))
    causal = live[:, None] & live[None, :] & (indices[None, :] <= indices[:, None])
    allowed = causal | (indices[:, None] == indices[None, :])
    return (positions, allowed)


def rope_tables(positions, head_width):
    half_width = head_width // 2
    frequency = jnp.exp(
        -jnp.log(rope_base) * (2.0 * jnp.arange(half_width, dtype=jnp.float32) / head_width)
    )
    angles = positions.astype(jnp.float32)[:, None] * frequency[None, :]
    return (jnp.cos(angles), jnp.sin(angles))


def rotate(values, cosine, sine_part):
    half_width = values.shape[-1] // 2
    first, second = (values[..., :half_width], values[..., half_width:])
    return jnp.concatenate(
        [first * cosine - second * sine_part, second * cosine + first * sine_part], axis=-1
    )


def rotate_back(grads, cosine, sine_part):
    half_width = grads.shape[-1] // 2
    first, second = (grads[..., :half_width], grads[..., half_width:])
    return jnp.concatenate(
        [first * cosine + second * sine_part, second * cosine - first * sine_part], axis=-1
    )


def product_t(left, right):
    return lax.dot_general(
        left, right, (((1,), (1,)), ((), ())), preferred_element_type=jnp.float32
    )


def product_tn(left, right):
    return lax.dot_general(
        left, right, (((0,), (0,)), ((), ())), preferred_element_type=jnp.float32
    )


def split_dims(count):
    return (count // 8, 2, 2, 2)


PAIR = 1
INNER = ((0, 2, 3), (0, 3, 2))


def pieces(layouts):
    chunks = []
    for out_index, members in enumerate(layouts):
        column = 0
        for index, half in members:
            parts = 2 if half % 256 == 0 else 1
            step = half // parts
            for part in range(parts):
                order = INNER[len(chunks) % len(INNER)]
                chunks.append((index, part * step, step, out_index, column + part * step, order))
            column += half
    return chunks


class Place:
    def __init__(self, sizes):
        self.sizes = sizes
        self.me = lax.axis_index("dp")
        self.strides = [math.prod(sizes[i + 1 :]) for i in range(len(sizes))]
        self.coords = [
            lax.rem(lax.div(self.me, stride), size) for stride, size in zip(self.strides, sizes)
        ]
        self.base = [sum(size - 1 for size in sizes[:i]) for i in range(len(sizes))]

    def other(self, dim, offset):
        return lax.rem(self.coords[dim] + offset, self.sizes[dim])

    def peer(self, dim, offset):
        return self.me + (self.other(dim, offset) - self.coords[dim]) * self.strides[dim]

    def slot(self, dim, offset):
        return self.base[dim] + offset - 1

    def barrier(self, extra=()):
        barrier = pltpu.get_barrier_semaphore()
        count = 0
        for dim, size in enumerate(self.sizes):
            for offset in range(1, size):
                pl.semaphore_signal(
                    barrier, inc=1, device_id={"dp": self.peer(dim, offset)}, device_id_type=MESH
                )
                count += 1
        for target in extra:
            pl.semaphore_signal(barrier, inc=1, device_id=target, device_id_type=MESH)
            count += 1
        pl.semaphore_wait(barrier, count)


def remote(source, target, send, recv, device):
    return pltpu.make_async_remote_copy(
        src_ref=source,
        dst_ref=target,
        send_sem=send,
        recv_sem=recv,
        device_id=device,
        device_id_type=MESH,
    )


def gather_kernel(sizes, chunks, counts, *refs):
    n_in, n_out, n_rows = counts
    refs = list(refs)
    ins = [refs.pop(0) for _ in range(n_in)]
    row_ins = [refs.pop(0) for _ in range(n_rows)]
    length_in = refs.pop(0)
    outs = [refs.pop(0) for _ in range(n_out)]
    row_outs = [refs.pop(0) for _ in range(n_rows)]
    length_out = refs.pop(0)
    send_sem, recv_sem, local_sem, row_send, row_recv, length_sem = refs
    place = Place(sizes)
    k = len(sizes)
    mine = place.coords[PAIR]
    theirs = place.other(PAIR, 1)
    tensor_me = lax.axis_index("tensor")
    near = {"tensor": 1 - tensor_me}
    far = {"dp": place.peer(PAIR, 1)}

    def region(chunk, done, dim=None, coord=None):
        where = []
        for i in range(k):
            if i == dim:
                where.append(coord)
            elif i in done:
                where.append(slice(None))
            else:
                where.append(place.coords[i])
        return outs[chunk[3]].at[tuple(where) + (slice(None), pl.ds(chunk[4], chunk[2]))]

    def source_of(chunk, half_index):
        half = ins[chunk[0]].shape[1] // 2
        start = pl.multiple_of(half_index * half + chunk[1], 128)
        return ins[chunk[0]].at[:, pl.ds(start, chunk[2])]

    def steps(chunk):
        return (PAIR,) + chunk[5]

    def sends(j, stage):
        chunk = chunks[j]
        order = steps(chunk)
        dim, done = order[stage], order[:stage]
        block = region(chunk, done)
        source = source_of(chunk, theirs) if stage == 0 else block
        return [
            remote(
                source,
                block,
                send_sem.at[j, place.slot(dim, offset)],
                recv_sem.at[j, place.slot(dim, offset)],
                {"dp": place.peer(dim, offset)},
            )
            for offset in range(1, sizes[dim])
        ]

    def wait_arrivals(j, stage):
        chunk = chunks[j]
        order = steps(chunk)
        dim, done = order[stage], order[:stage]
        for offset in range(1, sizes[dim]):
            block = region(chunk, done, dim, place.other(dim, sizes[dim] - offset))
            remote(
                block,
                block,
                send_sem.at[j, place.slot(dim, offset)],
                recv_sem.at[j, place.slot(dim, offset)],
                {"dp": place.peer(dim, offset)},
            ).wait_recv()

    place.barrier([near])
    started, own = [], []
    crossing = remote(
        length_in, length_out.at[mine], length_sem.at[0], length_sem.at[1], far
    )
    crossing.start()
    rows_far, rows_near = [], []
    for i in range(n_rows):
        slot = row_outs[i].at[mine, tensor_me]
        rows_far.append(remote(row_ins[i], slot, row_send.at[i, 0], row_recv.at[i, 0], far))
        rows_near.append(remote(row_ins[i], slot, row_send.at[i, 1], row_recv.at[i, 1], near))
        rows_far[-1].start()
        rows_near[-1].start()
    for j, chunk in enumerate(chunks):
        copies = sends(j, 0)
        for copy in copies:
            copy.start()
        started += copies
        copy = pltpu.make_async_copy(source_of(chunk, mine), region(chunk, ()), local_sem.at[j])
        copy.start()
        own.append(copy)
    length_out[mine] = length_in[...]
    passed = []
    for i in range(n_rows):
        row_outs[i][mine, tensor_me] = row_ins[i][...]
        rows_far[i].wait()
        slot = row_outs[i].at[theirs, tensor_me]
        passed.append(remote(slot, slot, row_send.at[i, 2], row_recv.at[i, 2], near))
        passed[-1].start()
    for step in range(len(chunks) + k - 1):
        for stage in range(1, k + 1):
            j = step - (stage - 1)
            if not 0 <= j < len(chunks):
                continue
            if stage == 1:
                own[j].wait()
            wait_arrivals(j, stage - 1)
            if stage < k:
                copies = sends(j, stage)
                for copy in copies:
                    copy.start()
                started += copies
    crossing.wait()
    for copy in rows_near + passed:
        copy.wait()
    for copy in started:
        copy.wait_send()


def gather_all(weights, layouts, rows, length_row, collective_id):
    sizes = split_dims(lax.axis_size("dp"))
    chunks = pieces(layouts)
    peers = sum(size - 1 for size in sizes)
    n_in, n_out, n_rows = len(weights), len(layouts), len(rows)
    depth = weights[0].shape[0]
    whole = pl.BlockSpec(memory_space=pltpu.VMEM)
    outs = pl.pallas_call(
        functools.partial(gather_kernel, sizes, chunks, (n_in, n_out, n_rows)),
        out_shape=[
            jax.ShapeDtypeStruct(sizes + (depth, sum(half for _, half in members)), jnp.bfloat16)
            for members in layouts
        ]
        + [jax.ShapeDtypeStruct((2, 2) + r.shape, r.dtype) for r in rows]
        + [jax.ShapeDtypeStruct((2,) + length_row.shape, length_row.dtype)],
        in_specs=[whole] * (n_in + n_rows + 1),
        out_specs=[pl.BlockSpec(memory_space=pl.ANY)] * n_out + [whole] * (n_rows + 1),
        scratch_shapes=[
            pltpu.SemaphoreType.DMA((len(chunks), peers)),
            pltpu.SemaphoreType.DMA((len(chunks), peers)),
            pltpu.SemaphoreType.DMA((len(chunks),)),
            pltpu.SemaphoreType.DMA((n_rows, 3)),
            pltpu.SemaphoreType.DMA((n_rows, 3)),
            pltpu.SemaphoreType.DMA((2,)),
        ],
        compiler_params=pltpu.CompilerParams(
            collective_id=collective_id, has_side_effects=True, vmem_limit_bytes=VMEM_LIMIT
        ),
    )(*weights, *rows, length_row)
    full = [out.reshape(-1, out.shape[-1]) for out in outs[:n_out]]
    row_sets = [out.reshape(-1, out.shape[-1]) for out in outs[n_out : n_out + n_rows]]
    return full, row_sets, outs[n_out + n_rows][:, 0, 0]


def reduce_kernel(sizes, chunks, counts, tensor_size, *refs):
    n_in, n_out = counts
    refs = list(refs)
    ins = [refs.pop(0) for _ in range(n_in)]
    gains = refs.pop(0)
    outs = [refs.pop(0) for _ in range(n_out)]
    gain_out = refs.pop(0)
    k = len(sizes)
    m = k - 1
    held = [[refs.pop(0) for _ in range(m - 1)] for _ in chunks]
    landed = [[refs.pop(0) for _ in range(m)] for _ in chunks]
    crossed = [refs.pop(0) for _ in chunks]
    gain_held = [refs.pop(0) for _ in range(k)]
    gain_landed = [refs.pop(0) for _ in range(k + 1)]
    send_sem, recv_sem, local_sem, gain_send, gain_recv = refs
    place = Place(sizes)
    tensor_me = lax.axis_index("tensor")
    mine = place.coords[PAIR]
    theirs = place.other(PAIR, 1)
    rows = ins[0].shape[-2]

    def order_of(j):
        return tuple(reversed(chunks[j][5]))

    def part(ref, dims, dim, coord, columns):
        where = tuple(coord if i == dim else slice(None) for i in dims)
        return ref.at[where + (slice(None), columns)]

    def copies_of(j, stage):
        _, _, width, array, column, _ = chunks[j]
        order = order_of(j)
        dim = order[stage]
        dims = [i for i in range(k) if i not in order[:stage]]
        if stage == 0:
            ref, columns = ins[array], pl.ds(column, width)
        else:
            ref, columns = held[j][stage - 1], slice(None)
        return [
            remote(
                part(ref, dims, dim, place.other(dim, offset), columns),
                landed[j][stage].at[offset - 1],
                send_sem.at[j, place.slot(dim, offset)],
                recv_sem.at[j, place.slot(dim, offset)],
                {"dp": place.peer(dim, offset)},
            )
            for offset in range(1, sizes[dim])
        ]

    def result_at(j):
        index, start, width = chunks[j][:3]
        half = outs[index].shape[1] // 2
        return outs[index], pl.ds(pl.multiple_of(mine * half + start, 128), width)

    def cross_copy(j):
        out, columns = result_at(j)
        slot = place.slot(PAIR, 1)
        return remote(
            crossed[j],
            out.at[:, columns],
            send_sem.at[j, slot],
            recv_sem.at[j, slot],
            {"dp": place.peer(PAIR, 1)},
        )

    def add_up(j, stage):
        order = order_of(j)
        dim = order[stage]
        dims = [i for i in range(k) if i not in order[:stage]]
        lead = [sizes[i] for i in dims if i != dim]
        per = rows // 16

        def total_of(where, rows_at):
            if stage == 0:
                own = tuple(where)
                source = held[j][0]
            else:
                own = list(where)
                own.insert(dims.index(dim), place.coords[dim])
                own = tuple(own)
                source = held[j][stage - 1]
            total = source[own + (rows_at, slice(None))].astype(jnp.float32)
            for offset in range(1, sizes[dim]):
                got = landed[j][stage][(offset - 1,) + tuple(where) + (rows_at, slice(None))]
                total = total + got.astype(jnp.float32)
            return total

        if stage == m - 1:

            def last(i, carry):
                rows_at = pl.ds(pl.multiple_of(i * 16, 16), 16)
                crossed[j][rows_at, :] = total_of((theirs,), rows_at)
                return carry

            lax.fori_loop(0, per, last, 0)
            copy = cross_copy(j)
            copy.start()

            def keep(i, carry):
                rows_at = pl.ds(pl.multiple_of(i * 16, 16), 16)
                out, columns = result_at(j)
                out[rows_at, columns] = total_of((mine,), rows_at)
                return carry

            lax.fori_loop(0, per, keep, 0)
            return copy

        def body(i, carry):
            rows_at = pl.ds(pl.multiple_of(lax.rem(i, per) * 16, 16), 16)
            flat = lax.div(i, per)
            where = []
            for position in range(len(lead)):
                below = math.prod(lead[position + 1 :])
                where.append(lax.rem(lax.div(flat, below), lead[position]))
            total = total_of(where, rows_at)
            held[j][stage][tuple(where) + (rows_at, slice(None))] = total.astype(jnp.bfloat16)
            return carry

        lax.fori_loop(0, math.prod(lead) * per, body, 0)
        return None

    def gain_copies(stage):
        source = gains if stage == 0 else gain_held[stage - 1]
        result = []
        if stage < k:
            for offset in range(1, sizes[stage]):
                slot = place.slot(stage, offset)
                result.append(
                    remote(
                        source,
                        gain_landed[stage].at[offset - 1],
                        gain_send.at[slot],
                        gain_recv.at[slot],
                        {"dp": place.peer(stage, offset)},
                    )
                )
        else:
            first = sum(size - 1 for size in sizes)
            for offset in range(1, tensor_size):
                result.append(
                    remote(
                        source,
                        gain_landed[stage].at[offset - 1],
                        gain_send.at[first + offset - 1],
                        gain_recv.at[first + offset - 1],
                        {"tensor": lax.rem(tensor_me + offset, tensor_size)},
                    )
                )
        return result

    place.barrier(
        [{"tensor": lax.rem(tensor_me + i, tensor_size)} for i in range(1, tensor_size)]
    )
    flights, own, crossing = [], [], []
    for j, chunk in enumerate(chunks):
        _, _, width, array, column, _ = chunk
        first = copies_of(j, 0)
        for copy in first:
            copy.start()
        flights.append([first])
        dim = order_of(j)[0]
        copy = pltpu.make_async_copy(
            part(ins[array], range(k), dim, place.coords[dim], pl.ds(column, width)),
            held[j][0],
            local_sem.at[j],
        )
        copy.start()
        own.append(copy)
        if j == 0:
            gain_flight = gain_copies(0)
            for copy in gain_flight:
                copy.start()
    for step in range(len(chunks) + m - 1):
        if step <= k:
            for copy in gain_flight:
                copy.wait()
            total = (gains if step == 0 else gain_held[step - 1])[...]
            for i in range(len(gain_flight)):
                total = total + gain_landed[step][i]
            if step < k:
                gain_held[step][...] = total
                gain_flight = gain_copies(step + 1)
                for copy in gain_flight:
                    copy.start()
            else:
                gain_out[...] = total
        for stage in range(m):
            j = step - stage
            if not 0 <= j < len(chunks):
                continue
            if stage == 0:
                own[j].wait()
            for copy in flights[j][stage]:
                copy.wait_recv()
            copy = add_up(j, stage)
            if stage < m - 1:
                following = copies_of(j, stage + 1)
                for copy in following:
                    copy.start()
                flights[j].append(following)
            else:
                crossing.append(copy)
    for copy in crossing:
        copy.wait_recv()
    for flight in flights:
        for copies in flight:
            for copy in copies:
                copy.wait_send()
    for copy in crossing:
        copy.wait_send()


def reduce_weights(grads, layouts, widths, gains, collective_id):
    sizes = split_dims(lax.axis_size("dp"))
    tensor_size = lax.axis_size("tensor")
    k = len(sizes)
    m = k - 1
    rows = grads[0].shape[0] // math.prod(sizes)
    chunks = pieces(layouts)
    peers = sum(size - 1 for size in sizes)
    n_in, n_out = len(grads), len(widths)
    held, landed, crossed = [], [], []
    for _, _, width, _, _, gather_order in chunks:
        order = tuple(reversed(gather_order))
        for stage in range(m):
            left = tuple(sizes[i] for i in range(k) if i not in order[: stage + 1])
            if stage < m - 1:
                held.append(pltpu.VMEM(left + (rows, width), jnp.bfloat16))
            landed.append(pltpu.VMEM((sizes[order[stage]] - 1,) + left + (rows, width), jnp.bfloat16))
        crossed.append(pltpu.VMEM((rows, width), jnp.float32))
    gain_landed = [pltpu.VMEM((size - 1,) + gains.shape, jnp.float32) for size in sizes + (tensor_size,)]
    whole = pl.BlockSpec(memory_space=pltpu.VMEM)
    outs = pl.pallas_call(
        functools.partial(reduce_kernel, sizes, chunks, (n_in, n_out), tensor_size),
        out_shape=[jax.ShapeDtypeStruct((rows, width), jnp.float32) for width in widths]
        + [jax.ShapeDtypeStruct(gains.shape, jnp.float32)],
        in_specs=[pl.BlockSpec(memory_space=pl.ANY)] * n_in + [whole],
        out_specs=[whole] * (n_out + 1),
        scratch_shapes=held
        + landed
        + crossed
        + [pltpu.VMEM(gains.shape, jnp.float32)] * k
        + gain_landed
        + [
            pltpu.SemaphoreType.DMA((len(chunks), peers)),
            pltpu.SemaphoreType.DMA((len(chunks), peers)),
            pltpu.SemaphoreType.DMA((len(chunks),)),
            pltpu.SemaphoreType.DMA((peers + tensor_size - 1,)),
            pltpu.SemaphoreType.DMA((peers + tensor_size - 1,)),
        ],
        compiler_params=pltpu.CompilerParams(
            collective_id=collective_id, has_side_effects=True, vmem_limit_bytes=VMEM_LIMIT
        ),
    )(*[g.reshape(sizes + (rows, g.shape[1])) for g in grads], gains)
    return outs[:n_out], outs[n_out]


def group_place():
    sizes = split_dims(lax.axis_size("dp"))
    place = Place(sizes)
    tensor_me = lax.axis_index("tensor")
    near = {"tensor": 1 - tensor_me}
    far = {"dp": place.peer(PAIR, 1)}
    return place.coords[PAIR], place.other(PAIR, 1), tensor_me, near, far


def group_barrier(near, far):
    barrier = pltpu.get_barrier_semaphore()
    pl.semaphore_signal(barrier, inc=1, device_id=near, device_id_type=MESH)
    pl.semaphore_signal(barrier, inc=1, device_id=far, device_id_type=MESH)
    pl.semaphore_wait(barrier, 2)


def gather_rows_kernel(in_ref, out_ref, send_sem, recv_sem):
    mine, theirs, tensor_me, near, far = group_place()
    group_barrier(near, far)
    rows = in_ref.shape[0] // 2
    across, beside, passed = [], [], []
    for i in range(2):
        source = in_ref.at[pl.ds(i * rows, rows)]
        slot = out_ref.at[mine, tensor_me, pl.ds(i * rows, rows)]
        across.append(remote(source, slot, send_sem.at[0, i], recv_sem.at[0, i], far))
        beside.append(remote(source, slot, send_sem.at[1, i], recv_sem.at[1, i], near))
        across[-1].start()
        beside[-1].start()
    out_ref[mine, tensor_me] = in_ref[...]
    for i in range(2):
        across[i].wait()
        slot = out_ref.at[theirs, tensor_me, pl.ds(i * rows, rows)]
        passed.append(remote(slot, slot, send_sem.at[2, i], recv_sem.at[2, i], near))
        passed[-1].start()
    for copy in beside + passed:
        copy.wait()


def gather_rows(values, collective_id):
    out = pl.pallas_call(
        gather_rows_kernel,
        out_shape=jax.ShapeDtypeStruct((2, 2) + values.shape, values.dtype),
        in_specs=[pl.BlockSpec(memory_space=pltpu.VMEM)],
        out_specs=pl.BlockSpec(memory_space=pltpu.VMEM),
        scratch_shapes=[pltpu.SemaphoreType.DMA((3, 2))] * 2,
        compiler_params=pltpu.CompilerParams(collective_id=collective_id, has_side_effects=True),
    )(values)
    return out.reshape(-1, values.shape[-1])


def scatter_rows_kernel(count, *refs):
    refs = list(refs)
    ins = [refs.pop(0) for _ in range(count)]
    outs = [refs.pop(0) for _ in range(count)]
    landed = [refs.pop(0) for _ in range(count)]
    sent = [refs.pop(0) for _ in range(count)]
    got = [refs.pop(0) for _ in range(count)]
    send_sem, recv_sem = refs
    mine, theirs, tensor_me, near, far = group_place()
    group_barrier(near, far)
    parts = 2
    rows = outs[0].shape[0] // parts
    first, second, across = [], [], []

    def span(part):
        return pl.ds(part * rows, rows)

    for i in range(count):
        for part in range(parts):
            copy = remote(
                ins[i].at[theirs, 1 - tensor_me, span(part)],
                landed[i].at[0, span(part)],
                send_sem.at[i, 0, part],
                recv_sem.at[i, 0, part],
                near,
            )
            copy.start()
            first.append(copy)
        copy = remote(
            ins[i].at[mine, 1 - tensor_me],
            landed[i].at[1],
            send_sem.at[i, 1, 0],
            recv_sem.at[i, 1, 0],
            near,
        )
        copy.start()
        second.append(copy)
    for i in range(count):
        for part in range(parts):
            first[i * parts + part].wait_recv()

            def body(r, carry):
                at = pl.ds(pl.multiple_of(part * rows + r * 16, 16), 16)
                total = ins[i][theirs, tensor_me, at, :] + landed[i][0, at, :]
                sent[i][at, :] = total.astype(jnp.bfloat16)
                return carry

            lax.fori_loop(0, rows // 16, body, 0)
            copy = remote(
                sent[i].at[span(part)],
                got[i].at[span(part)],
                send_sem.at[i, 2, part],
                recv_sem.at[i, 2, part],
                far,
            )
            copy.start()
            across.append(copy)
    for i in range(count):
        second[i].wait_recv()
        for part in range(parts):
            across[i * parts + part].wait_recv()

            def body(r, carry):
                at = pl.ds(pl.multiple_of(part * rows + r * 16, 16), 16)
                total = ins[i][mine, tensor_me, at, :] + landed[i][1, at, :]
                outs[i][at, :] = total + got[i][at, :].astype(jnp.float32)
                return carry

            lax.fori_loop(0, rows // 16, body, 0)
    for copy in first + second + across:
        copy.wait_send()


def scatter_rows(partials, collective_id):
    count = len(partials)
    rows, width = partials[0].shape[0] // 4, partials[0].shape[1]
    whole = pl.BlockSpec(memory_space=pltpu.VMEM)
    return pl.pallas_call(
        functools.partial(scatter_rows_kernel, count),
        out_shape=[jax.ShapeDtypeStruct((rows, width), jnp.float32)] * count,
        in_specs=[whole] * count,
        out_specs=[whole] * count,
        scratch_shapes=[pltpu.VMEM((2, rows, width), jnp.float32)] * count
        + [pltpu.VMEM((rows, width), jnp.bfloat16)] * (2 * count)
        + [pltpu.SemaphoreType.DMA((count, 3, 2))] * 2,
        compiler_params=pltpu.CompilerParams(
            collective_id=collective_id, has_side_effects=True, vmem_limit_bytes=VMEM_LIMIT
        ),
    )(*[p.reshape(2, 2, rows, width) for p in partials])


def masked_scores(query_rot, key_rot, allowed, scaling):
    scores = (
        jnp.einsum("sqgrd,skgd->sgrqk", query_rot, key_rot, preferred_element_type=jnp.float32)
        * scaling
    )
    return jnp.where(allowed[:, None, None], scores, -1e30)


def per_device(
    tokens,
    cotangent,
    lengths,
    w_query,
    key_matrix,
    value_matrix,
    w_out,
    w_gate,
    w_up,
    w_down,
    gain_attn,
    gain_mlp,
    gain_query,
    gain_key,
):
    own_rows = tokens.shape[0]
    total_rows = own_rows * 2
    weights = (w_query, key_matrix, value_matrix, w_out, w_gate, w_up, w_down)
    halves = [w.shape[1] // 2 for w in weights]
    layouts = (
        ((0, halves[0]), (1, halves[1]), (2, halves[2])),
        ((3, halves[3]),),
        ((4, halves[4]), (5, halves[5])),
        ((6, halves[6]),),
    )
    own_index = lax.axis_index("tensor") * own_rows + jnp.arange(own_rows, dtype=jnp.int32)
    own_live = own_index < lengths[0]
    cot_live = jnp.where(own_live[:, None], cotangent, jnp.zeros_like(cotangent))
    scaling = HEAD_SIZE ** (-0.5)
    group_ratio = QUERY_HEADS // KEY_VALUE_HEADS
    token_values = tokens.astype(jnp.float32)
    attn_norm, attn_inverse = rms_rows(token_values, gain_attn)
    length_row = jnp.broadcast_to(lengths.astype(jnp.float32)[:, None], (8, HEAD_SIZE))
    fetched, row_sets, length_pair = gather_all(
        weights, layouts, (attn_norm.astype(jnp.bfloat16), cot_live), length_row, 0
    )
    full_qkv, full_out, full_gu, full_down = fetched
    normed, grad_result = row_sets
    positions, allowed = jax.vmap(lambda n: layout(n, total_rows))(length_pair.astype(jnp.int32))
    cosine, sine_part = rope_tables(positions.reshape(-1), HEAD_SIZE)
    cosine, sine_part = (t.reshape(2, total_rows, -1) for t in (cosine, sine_part))
    cos_query, sin_query = (cosine[:, :, None, None, :], sine_part[:, :, None, None, :])
    cos_key, sin_key = (cosine[:, :, None, :], sine_part[:, :, None, :])
    kv_heads = halves[1] // HEAD_SIZE
    q_end, k_end = halves[0], halves[0] + halves[1]
    qkv = jnp.dot(normed, full_qkv, preferred_element_type=jnp.float32)
    query_raw = qkv[:, :q_end].reshape(2, total_rows, kv_heads, group_ratio, HEAD_SIZE)
    key_raw = qkv[:, q_end:k_end].reshape(2, total_rows, kv_heads, HEAD_SIZE)
    value_part = qkv[:, k_end:].astype(jnp.bfloat16).reshape(2, total_rows, kv_heads, HEAD_SIZE)
    query_normed, query_inverse = rms_rows(query_raw, gain_query)
    key_normed, key_inverse = rms_rows(key_raw, gain_key)
    query_rot = rotate(query_normed, cos_query, sin_query).astype(jnp.bfloat16)
    key_rot = rotate(key_normed, cos_key, sin_key).astype(jnp.bfloat16)
    scores = masked_scores(query_rot, key_rot, allowed, scaling)
    row_max = jnp.max(scores, axis=-1, keepdims=True)
    log_total = row_max + jnp.log(jnp.sum(jnp.exp(scores - row_max), axis=-1, keepdims=True))
    attn_probs = jnp.exp(scores - log_total).astype(jnp.bfloat16)
    mixed = jnp.einsum(
        "sgrqk,skgd->sqgrd", attn_probs, value_part, preferred_element_type=jnp.float32
    ).astype(jnp.bfloat16)
    mixed_flat = mixed.reshape(2 * total_rows, -1)
    resid = token_values + scatter_rows([product_t(mixed_flat, full_out)], 7)[0]
    mlp_norm, mlp_inverse = rms_rows(resid, gain_mlp)
    mlp_in = gather_rows(mlp_norm.astype(jnp.bfloat16), 4)
    gate_up = jnp.dot(mlp_in, full_gu, preferred_element_type=jnp.float32)
    gate_proj, up_proj = gate_up[:, : halves[4]], gate_up[:, halves[4] :]
    activation = (jax.nn.silu(gate_proj) * up_proj).astype(jnp.bfloat16)
    grad_act = jnp.dot(grad_result, full_down, preferred_element_type=jnp.float32)
    sigma = jax.nn.sigmoid(gate_proj)
    grad_gate = (grad_act * up_proj * sigma * (1.0 + gate_proj * (1.0 - sigma))).astype(
        jnp.bfloat16
    )
    grad_up = (grad_act * gate_proj * sigma).astype(jnp.bfloat16)
    grad_gu = jnp.concatenate([grad_gate, grad_up], axis=1)
    grad_mlp_in, down_rows = scatter_rows(
        [product_t(grad_gu, full_gu), product_t(activation, full_down)], 8
    )
    result = (resid + down_rows).astype(jnp.bfloat16)
    grad_w_down = product_tn(grad_result, activation)
    grad_w_gu = product_tn(mlp_in, grad_gu)
    grad_resid_mlp, grad_gain_mlp = rms_back(grad_mlp_in, resid, mlp_inverse, gain_mlp)
    grad_resid = cot_live.astype(jnp.float32) + grad_resid_mlp
    grad_attn = gather_rows(grad_resid.astype(jnp.bfloat16), 6)
    grad_w_out = product_tn(grad_attn, mixed_flat)
    grad_mixed = (
        jnp.dot(grad_attn, full_out, preferred_element_type=jnp.float32)
        .astype(jnp.bfloat16)
        .reshape(2, total_rows, kv_heads, group_ratio, HEAD_SIZE)
    )
    scores = masked_scores(query_rot, key_rot, allowed, scaling)
    probs_full = jnp.exp(scores - log_total)
    probs_half = probs_full.astype(jnp.bfloat16)
    grad_value = jnp.einsum(
        "sgrqk,sqgrd->skgd", probs_half, grad_mixed, preferred_element_type=jnp.float32
    )
    grad_probs = jnp.einsum(
        "sqgrd,skgd->sgrqk", grad_mixed, value_part, preferred_element_type=jnp.float32
    )
    row_delta = jnp.sum(grad_mixed.astype(jnp.float32) * mixed.astype(jnp.float32), axis=-1)
    row_delta = jnp.transpose(row_delta, (0, 2, 3, 1))[..., None]
    grad_scores = (probs_full * (grad_probs - row_delta) * scaling).astype(jnp.bfloat16)
    grad_query_rot = jnp.einsum(
        "sgrqk,skgd->sqgrd", grad_scores, key_rot, preferred_element_type=jnp.float32
    )
    grad_key_rot = jnp.einsum(
        "sgrqk,sqgrd->skgd", grad_scores, query_rot, preferred_element_type=jnp.float32
    )
    grad_query_raw, grad_gain_query = rms_back(
        rotate_back(grad_query_rot, cos_query, sin_query), query_raw, query_inverse, gain_query
    )
    grad_key_raw, grad_gain_key = rms_back(
        rotate_back(grad_key_rot, cos_key, sin_key), key_raw, key_inverse, gain_key
    )
    grad_qkv = jnp.concatenate(
        [
            part.astype(jnp.bfloat16).reshape(2 * total_rows, -1)
            for part in (grad_query_raw, grad_key_raw, grad_value)
        ],
        axis=1,
    )
    grad_w_qkv = product_tn(normed, grad_qkv)
    grad_normed = scatter_rows([product_t(grad_qkv, full_qkv)], 10)[0]
    grad_tokens_attn, grad_gain_attn = rms_back(grad_normed, token_values, attn_inverse, gain_attn)
    grad_tokens = grad_resid + grad_tokens_attn
    gain_parts = (grad_gain_attn, grad_gain_mlp, grad_gain_query, grad_gain_key)
    gain_rows = [part.reshape(-1, HEAD_SIZE) for part in gain_parts]
    used = sum(part.shape[0] for part in gain_rows)
    gain_rows.append(jnp.zeros((-used % 8, HEAD_SIZE), jnp.float32))
    weight_sums, gain_sum = reduce_weights(
        [g.astype(jnp.bfloat16) for g in (grad_w_qkv, grad_w_out, grad_w_gu, grad_w_down)],
        layouts,
        [w.shape[1] for w in weights],
        jnp.concatenate(gain_rows, axis=0),
        collective_id=1,
    )
    gain_totals, row = [], 0
    for part in gain_parts:
        taken = part.shape[0] // HEAD_SIZE
        gain_totals.append(gain_sum[row : row + taken].reshape(-1))
        row += taken
    return (result, grad_tokens, *weight_sums, *gain_totals)


def solution(mesh):
    in_specs = (
        P(("dp", "tensor"), None),
        P(("dp", "tensor"), None),
        P("dp"),
        P("dp", "tensor"),
        P("dp", "tensor"),
        P("dp", "tensor"),
        P("dp", "tensor"),
        P("dp", "tensor"),
        P("dp", "tensor"),
        P("dp", "tensor"),
        P(),
        P(),
        P(),
        P(),
    )
    out_specs = (
        P(("dp", "tensor"), None),
        P(("dp", "tensor"), None),
        P("dp", "tensor"),
        P("dp", "tensor"),
        P("dp", "tensor"),
        P("dp", "tensor"),
        P("dp", "tensor"),
        P("dp", "tensor"),
        P("dp", "tensor"),
        P(),
        P(),
        P(),
        P(),
    )
    return jax.shard_map(
        per_device, mesh=mesh, in_specs=in_specs, out_specs=out_specs, check_vma=False
    )
```

```python
import functools
import math

import jax
import jax.numpy as jnp
from jax import lax
from jax.experimental import pallas as pl
from jax.experimental.pallas import tpu as pltpu
from jax.sharding import PartitionSpec as P

MESH = pl.DeviceIdType.MESH
VMEM_LIMIT = 64000000

QUERY_HEADS = 16
KEY_VALUE_HEADS = 8
HEAD_SIZE = 128


norm_eps = 1e-06
rope_base = 1000000.0


def rms_rows(values, gain_vec):
    inverse = lax.rsqrt(jnp.mean(values * values, axis=-1, keepdims=True) + norm_eps)
    return (values * inverse * gain_vec, inverse)


def rms_back(grad_output, values, inverse, gain_vec):
    scaled = grad_output * gain_vec
    mean_term = jnp.mean(scaled * values, axis=-1, keepdims=True)
    grad_values = inverse * scaled - values * (inverse * inverse * inverse) * mean_term
    flat_terms = (grad_output * values * inverse).reshape(-1, values.shape[-1])
    return (grad_values, jnp.sum(flat_terms, axis=0))


def layout(length_value, total_rows):
    length_value = jnp.asarray(length_value)
    indices = jnp.arange(total_rows, dtype=jnp.int32)
    live = indices < length_value
    positions = jnp.where(live, indices, jnp.zeros_like(indices))
    causal = live[:, None] & live[None, :] & (indices[None, :] <= indices[:, None])
    allowed = causal | (indices[:, None] == indices[None, :])
    return (positions, allowed)


def rope_tables(positions, head_width):
    half_width = head_width // 2
    frequency = jnp.exp(
        -jnp.log(rope_base) * (2.0 * jnp.arange(half_width, dtype=jnp.float32) / head_width)
    )
    angles = positions.astype(jnp.float32)[:, None] * frequency[None, :]
    return (jnp.cos(angles), jnp.sin(angles))


def rotate(values, cosine, sine_part):
    half_width = values.shape[-1] // 2
    first, second = (values[..., :half_width], values[..., half_width:])
    return jnp.concatenate(
        [first * cosine - second * sine_part, second * cosine + first * sine_part], axis=-1
    )


def rotate_back(grads, cosine, sine_part):
    half_width = grads.shape[-1] // 2
    first, second = (grads[..., :half_width], grads[..., half_width:])
    return jnp.concatenate(
        [first * cosine + second * sine_part, second * cosine - first * sine_part], axis=-1
    )


def product_t(left, right):
    return lax.dot_general(
        left, right, (((1,), (1,)), ((), ())), preferred_element_type=jnp.float32
    )


def product_tn(left, right):
    return lax.dot_general(
        left, right, (((0,), (0,)), ((), ())), preferred_element_type=jnp.float32
    )


def split_dims(count):
    return (count // 8, 2, 2, 2)


PAIR = 1
AHEAD = 5
DEPTH = 2
RUN = 3
LAG = 2
INNER = ((0, 2, 3), (0, 3, 2))


def pieces(layouts):
    chunks = []
    for out_index, members in enumerate(layouts):
        column = 0
        for index, half in members:
            step = math.gcd(half, 256)
            parts = half // step
            for part in range(parts):
                order = INNER[len(chunks) % len(INNER)]
                chunks.append((index, part * step, step, out_index, column + part * step, order))
            column += half
    return chunks


class Place:
    def __init__(self, sizes):
        self.sizes = sizes
        self.me = lax.axis_index("dp")
        self.strides = [math.prod(sizes[i + 1 :]) for i in range(len(sizes))]
        self.coords = [
            lax.rem(lax.div(self.me, stride), size) for stride, size in zip(self.strides, sizes)
        ]
        self.base = [sum(size - 1 for size in sizes[:i]) for i in range(len(sizes))]

    def other(self, dim, offset):
        return lax.rem(self.coords[dim] + offset, self.sizes[dim])

    def peer(self, dim, offset):
        return self.me + (self.other(dim, offset) - self.coords[dim]) * self.strides[dim]

    def slot(self, dim, offset):
        return self.base[dim] + offset - 1

    def barrier(self, extra=()):
        barrier = pltpu.get_barrier_semaphore()
        count = 0
        for dim, size in enumerate(self.sizes):
            for offset in range(1, size):
                pl.semaphore_signal(
                    barrier, inc=1, device_id={"dp": self.peer(dim, offset)}, device_id_type=MESH
                )
                count += 1
        for target in extra:
            pl.semaphore_signal(barrier, inc=1, device_id=target, device_id_type=MESH)
            count += 1
        pl.semaphore_wait(barrier, count)


def remote(source, target, send, recv, device):
    return pltpu.make_async_remote_copy(
        src_ref=source,
        dst_ref=target,
        send_sem=send,
        recv_sem=recv,
        device_id=device,
        device_id_type=MESH,
    )


def gather_kernel(sizes, chunks, counts, *refs):
    n_in, n_out, n_rows = counts
    refs = list(refs)
    ins = [refs.pop(0) for _ in range(n_in)]
    row_ins = [refs.pop(0) for _ in range(n_rows)]
    length_in = refs.pop(0)
    outs = [refs.pop(0) for _ in range(n_out)]
    row_outs = [refs.pop(0) for _ in range(n_rows)]
    length_out = refs.pop(0)
    send_sem, recv_sem, local_sem, row_send, row_recv, length_sem = refs
    place = Place(sizes)
    k = len(sizes)
    mine = place.coords[PAIR]
    theirs = place.other(PAIR, 1)
    tensor_me = lax.axis_index("tensor")
    near = {"tensor": 1 - tensor_me}
    far = {"dp": place.peer(PAIR, 1)}

    def region(chunk, done, dim=None, coord=None):
        where = []
        for i in range(k):
            if i == dim:
                where.append(coord)
            elif i in done:
                where.append(slice(None))
            else:
                where.append(place.coords[i])
        return outs[chunk[3]].at[tuple(where) + (slice(None), pl.ds(chunk[4], chunk[2]))]

    def source_of(chunk, half_index):
        half = ins[chunk[0]].shape[1] // 2
        start = pl.multiple_of(half_index * half + chunk[1], 128)
        return ins[chunk[0]].at[:, pl.ds(start, chunk[2])]

    def steps(chunk):
        return (PAIR,) + chunk[5]

    def sends(j, stage):
        chunk = chunks[j]
        order = steps(chunk)
        dim, done = order[stage], order[:stage]
        block = region(chunk, done)
        source = source_of(chunk, theirs) if stage == 0 else block
        return [
            remote(
                source,
                block,
                send_sem.at[j, place.slot(dim, offset)],
                recv_sem.at[j, place.slot(dim, offset)],
                {"dp": place.peer(dim, offset)},
            )
            for offset in range(1, sizes[dim])
        ]

    def wait_arrivals(j, stage):
        chunk = chunks[j]
        order = steps(chunk)
        dim, done = order[stage], order[:stage]
        for offset in range(1, sizes[dim]):
            block = region(chunk, done, dim, place.other(dim, sizes[dim] - offset))
            remote(
                block,
                block,
                send_sem.at[j, place.slot(dim, offset)],
                recv_sem.at[j, place.slot(dim, offset)],
                {"dp": place.peer(dim, offset)},
            ).wait_recv()

    place.barrier([near])
    started, own = [], []
    crossing = remote(
        length_in, length_out.at[mine], length_sem.at[0], length_sem.at[1], far
    )
    crossing.start()
    rows_far, rows_near, passed = [], [], []

    def send_rows(i):
        slot = row_outs[i].at[mine, tensor_me]
        rows_far.append(remote(row_ins[i], slot, row_send.at[i, 0], row_recv.at[i, 0], far))
        rows_near.append(remote(row_ins[i], slot, row_send.at[i, 1], row_recv.at[i, 1], near))
        rows_far[-1].start()
        rows_near[-1].start()
        row_outs[i][mine, tensor_me] = row_ins[i][...]

    def pass_rows(i):
        rows_far[i].wait()
        slot = row_outs[i].at[theirs, tensor_me]
        passed.append(remote(slot, slot, row_send.at[i, 2], row_recv.at[i, 2], near))
        passed[-1].start()

    def begin(j):
        copies = sends(j, 0)
        for copy in copies:
            copy.start()
        started.extend(copies)
        copy = pltpu.make_async_copy(
            source_of(chunks[j], mine), region(chunks[j], ()), local_sem.at[j]
        )
        copy.start()
        own.append(copy)

    for j in range(min(AHEAD, len(chunks))):
        begin(j)
    length_out[mine] = length_in[...]
    total_steps = len(chunks) + DEPTH * (k - 1)
    for step in range(total_steps):
        if step + AHEAD < len(chunks):
            begin(step + AHEAD)
        for i in range(n_rows):
            if step == min(4 + 3 * i, total_steps - 1):
                send_rows(i)
        for stage in range(k, 0, -1):
            j = step - DEPTH * (stage - 1)
            if not 0 <= j < len(chunks):
                continue
            if stage == 1:
                own[j].wait()
            wait_arrivals(j, stage - 1)
            if stage < k:
                copies = sends(j, stage)
                for copy in copies:
                    copy.start()
                started += copies
        for i in range(n_rows):
            if step == min(12 + i, total_steps - 1):
                pass_rows(i)
    crossing.wait()
    for copy in rows_near + passed:
        copy.wait()
    for copy in started:
        copy.wait_send()


def gather_all(weights, layouts, rows, length_row, collective_id):
    sizes = split_dims(lax.axis_size("dp"))
    chunks = pieces(layouts)
    peers = sum(size - 1 for size in sizes)
    n_in, n_out, n_rows = len(weights), len(layouts), len(rows)
    depth = weights[0].shape[0]
    whole = pl.BlockSpec(memory_space=pltpu.VMEM)
    outs = pl.pallas_call(
        functools.partial(gather_kernel, sizes, chunks, (n_in, n_out, n_rows)),
        out_shape=[
            jax.ShapeDtypeStruct(sizes + (depth, sum(half for _, half in members)), jnp.bfloat16)
            for members in layouts
        ]
        + [jax.ShapeDtypeStruct((2, 2) + r.shape, r.dtype) for r in rows]
        + [jax.ShapeDtypeStruct((2,) + length_row.shape, length_row.dtype)],
        in_specs=[whole] * (n_in + n_rows + 1),
        out_specs=[pl.BlockSpec(memory_space=pl.ANY)] * n_out + [whole] * (n_rows + 1),
        scratch_shapes=[
            pltpu.SemaphoreType.DMA((len(chunks), peers)),
            pltpu.SemaphoreType.DMA((len(chunks), peers)),
            pltpu.SemaphoreType.DMA((len(chunks),)),
            pltpu.SemaphoreType.DMA((n_rows, 3)),
            pltpu.SemaphoreType.DMA((n_rows, 3)),
            pltpu.SemaphoreType.DMA((2,)),
        ],
        compiler_params=pltpu.CompilerParams(
            collective_id=collective_id, has_side_effects=True, vmem_limit_bytes=VMEM_LIMIT
        ),
    )(*weights, *rows, length_row)
    full = [out.reshape(-1, out.shape[-1]) for out in outs[:n_out]]
    row_sets = [out.reshape(-1, out.shape[-1]) for out in outs[n_out : n_out + n_rows]]
    return full, row_sets, outs[n_out + n_rows][:, 0, 0]


def reduce_kernel(sizes, chunks, counts, tensor_size, *refs):
    n_in, n_out = counts
    refs = list(refs)
    ins = [refs.pop(0) for _ in range(n_in)]
    gains = refs.pop(0)
    outs = [refs.pop(0) for _ in range(n_out)]
    gain_out = refs.pop(0)
    k = len(sizes)
    m = k - 1
    held = [[refs.pop(0) for _ in range(m - 1)] for _ in chunks]
    landed = [[refs.pop(0) for _ in range(m)] for _ in chunks]
    crossed = [refs.pop(0) for _ in chunks]
    gain_held = [refs.pop(0) for _ in range(k)]
    gain_landed = [refs.pop(0) for _ in range(k + 1)]
    send_sem, recv_sem, local_sem, gain_send, gain_recv = refs
    place = Place(sizes)
    tensor_me = lax.axis_index("tensor")
    mine = place.coords[PAIR]
    theirs = place.other(PAIR, 1)
    rows = ins[0].shape[-2]

    def order_of(j):
        return tuple(reversed(chunks[j][5]))

    def part(ref, dims, dim, coord, columns):
        where = tuple(coord if i == dim else slice(None) for i in dims)
        return ref.at[where + (slice(None), columns)]

    def copies_of(j, stage):
        _, _, width, array, column, _ = chunks[j]
        order = order_of(j)
        dim = order[stage]
        dims = [i for i in range(k) if i not in order[:stage]]
        if stage == 0:
            ref, columns = ins[array], pl.ds(column, width)
        else:
            ref, columns = held[j][stage - 1], slice(None)
        return [
            remote(
                part(ref, dims, dim, place.other(dim, offset), columns),
                landed[j][stage].at[offset - 1],
                send_sem.at[j, place.slot(dim, offset)],
                recv_sem.at[j, place.slot(dim, offset)],
                {"dp": place.peer(dim, offset)},
            )
            for offset in range(1, sizes[dim])
        ]

    def result_at(j):
        index, start, width = chunks[j][:3]
        half = outs[index].shape[1] // 2
        return outs[index], pl.ds(pl.multiple_of(mine * half + start, 128), width)

    def cross_copy(j):
        out, columns = result_at(j)
        slot = place.slot(PAIR, 1)
        return remote(
            crossed[j],
            out.at[:, columns],
            send_sem.at[j, slot],
            recv_sem.at[j, slot],
            {"dp": place.peer(PAIR, 1)},
        )

    def add_up(j, stage):
        order = order_of(j)
        dim = order[stage]
        dims = [i for i in range(k) if i not in order[:stage]]
        lead = [sizes[i] for i in dims if i != dim]
        per = rows // 16

        def total_of(where, rows_at):
            if stage == 0:
                own = tuple(where)
                source = held[j][0]
            else:
                own = list(where)
                own.insert(dims.index(dim), place.coords[dim])
                own = tuple(own)
                source = held[j][stage - 1]
            total = source[own + (rows_at, slice(None))].astype(jnp.float32)
            for offset in range(1, sizes[dim]):
                got = landed[j][stage][(offset - 1,) + tuple(where) + (rows_at, slice(None))]
                total = total + got.astype(jnp.float32)
            return total

        if stage == m - 1:

            def last(i, carry):
                rows_at = pl.ds(pl.multiple_of(i * 16, 16), 16)
                crossed[j][rows_at, :] = total_of((theirs,), rows_at)
                return carry

            lax.fori_loop(0, per, last, 0)
            copy = cross_copy(j)
            copy.start()

            def keep(i, carry):
                rows_at = pl.ds(pl.multiple_of(i * 16, 16), 16)
                out, columns = result_at(j)
                out[rows_at, columns] = total_of((mine,), rows_at)
                return carry

            lax.fori_loop(0, per, keep, 0)
            return copy

        def body(i, carry):
            rows_at = pl.ds(pl.multiple_of(lax.rem(i, per) * 16, 16), 16)
            flat = lax.div(i, per)
            where = []
            for position in range(len(lead)):
                below = math.prod(lead[position + 1 :])
                where.append(lax.rem(lax.div(flat, below), lead[position]))
            total = total_of(where, rows_at)
            held[j][stage][tuple(where) + (rows_at, slice(None))] = total.astype(jnp.bfloat16)
            return carry

        lax.fori_loop(0, math.prod(lead) * per, body, 0)
        return None

    def gain_copies(stage):
        source = gains if stage == 0 else gain_held[stage - 1]
        result = []
        if stage < k:
            for offset in range(1, sizes[stage]):
                slot = place.slot(stage, offset)
                result.append(
                    remote(
                        source,
                        gain_landed[stage].at[offset - 1],
                        gain_send.at[slot],
                        gain_recv.at[slot],
                        {"dp": place.peer(stage, offset)},
                    )
                )
        else:
            first = sum(size - 1 for size in sizes)
            for offset in range(1, tensor_size):
                result.append(
                    remote(
                        source,
                        gain_landed[stage].at[offset - 1],
                        gain_send.at[first + offset - 1],
                        gain_recv.at[first + offset - 1],
                        {"tensor": lax.rem(tensor_me + offset, tensor_size)},
                    )
                )
        return result

    place.barrier(
        [{"tensor": lax.rem(tensor_me + i, tensor_size)} for i in range(1, tensor_size)]
    )
    flights, own, crossing = [], [], []

    def begin(j):
        _, _, width, array, column, _ = chunks[j]
        first = copies_of(j, 0)
        for copy in first:
            copy.start()
        flights.append([first])
        dim = order_of(j)[0]
        copy = pltpu.make_async_copy(
            part(ins[array], range(k), dim, place.coords[dim], pl.ds(column, width)),
            held[j][0],
            local_sem.at[j],
        )
        copy.start()
        own.append(copy)

    for j in range(min(RUN, len(chunks))):
        begin(j)
    gain_flight = gain_copies(0)
    for copy in gain_flight:
        copy.start()
    for step in range(len(chunks) + LAG * (m - 1)):
        if step + RUN < len(chunks):
            begin(step + RUN)
        if step % 2 == 1 and step // 2 <= k:
            turn = step // 2
            for copy in gain_flight:
                copy.wait()
            total = (gains if turn == 0 else gain_held[turn - 1])[...]
            for i in range(len(gain_flight)):
                total = total + gain_landed[turn][i]
            if turn < k:
                gain_held[turn][...] = total
                gain_flight = gain_copies(turn + 1)
                for copy in gain_flight:
                    copy.start()
            else:
                gain_out[...] = total
        for stage in range(m - 1, -1, -1):
            j = step - LAG * stage
            if not 0 <= j < len(chunks):
                continue
            if stage == 0:
                own[j].wait()
            for copy in flights[j][stage]:
                copy.wait_recv()
            copy = add_up(j, stage)
            if stage < m - 1:
                following = copies_of(j, stage + 1)
                for copy in following:
                    copy.start()
                flights[j].append(following)
            else:
                crossing.append(copy)
    for copy in crossing:
        copy.wait_recv()
    for flight in flights:
        for copies in flight:
            for copy in copies:
                copy.wait_send()
    for copy in crossing:
        copy.wait_send()


def reduce_weights(grads, layouts, widths, gains, collective_id):
    sizes = split_dims(lax.axis_size("dp"))
    tensor_size = lax.axis_size("tensor")
    k = len(sizes)
    m = k - 1
    rows = grads[0].shape[0] // math.prod(sizes)
    chunks = pieces(layouts)
    peers = sum(size - 1 for size in sizes)
    n_in, n_out = len(grads), len(widths)
    held, landed, crossed = [], [], []
    for _, _, width, _, _, gather_order in chunks:
        order = tuple(reversed(gather_order))
        for stage in range(m):
            left = tuple(sizes[i] for i in range(k) if i not in order[: stage + 1])
            if stage < m - 1:
                held.append(pltpu.VMEM(left + (rows, width), jnp.bfloat16))
            landed.append(pltpu.VMEM((sizes[order[stage]] - 1,) + left + (rows, width), jnp.bfloat16))
        crossed.append(pltpu.VMEM((rows, width), jnp.float32))
    gain_landed = [pltpu.VMEM((size - 1,) + gains.shape, jnp.float32) for size in sizes + (tensor_size,)]
    whole = pl.BlockSpec(memory_space=pltpu.VMEM)
    outs = pl.pallas_call(
        functools.partial(reduce_kernel, sizes, chunks, (n_in, n_out), tensor_size),
        out_shape=[jax.ShapeDtypeStruct((rows, width), jnp.float32) for width in widths]
        + [jax.ShapeDtypeStruct(gains.shape, jnp.float32)],
        in_specs=[pl.BlockSpec(memory_space=pl.ANY)] * n_in + [whole],
        out_specs=[whole] * (n_out + 1),
        scratch_shapes=held
        + landed
        + crossed
        + [pltpu.VMEM(gains.shape, jnp.float32)] * k
        + gain_landed
        + [
            pltpu.SemaphoreType.DMA((len(chunks), peers)),
            pltpu.SemaphoreType.DMA((len(chunks), peers)),
            pltpu.SemaphoreType.DMA((len(chunks),)),
            pltpu.SemaphoreType.DMA((peers + tensor_size - 1,)),
            pltpu.SemaphoreType.DMA((peers + tensor_size - 1,)),
        ],
        compiler_params=pltpu.CompilerParams(
            collective_id=collective_id, has_side_effects=True, vmem_limit_bytes=VMEM_LIMIT
        ),
    )(*[g.reshape(sizes + (rows, g.shape[1])) for g in grads], gains)
    return outs[:n_out], outs[n_out]


def group_place():
    sizes = split_dims(lax.axis_size("dp"))
    place = Place(sizes)
    tensor_me = lax.axis_index("tensor")
    near = {"tensor": 1 - tensor_me}
    far = {"dp": place.peer(PAIR, 1)}
    return place.coords[PAIR], place.other(PAIR, 1), tensor_me, near, far


def group_barrier(near, far):
    barrier = pltpu.get_barrier_semaphore()
    pl.semaphore_signal(barrier, inc=1, device_id=near, device_id_type=MESH)
    pl.semaphore_signal(barrier, inc=1, device_id=far, device_id_type=MESH)
    pl.semaphore_wait(barrier, 2)


def gather_rows_kernel(in_ref, out_ref, send_sem, recv_sem):
    mine, theirs, tensor_me, near, far = group_place()
    group_barrier(near, far)
    rows = in_ref.shape[0] // 2
    across, beside, passed = [], [], []
    for i in range(2):
        source = in_ref.at[pl.ds(i * rows, rows)]
        slot = out_ref.at[mine, tensor_me, pl.ds(i * rows, rows)]
        across.append(remote(source, slot, send_sem.at[0, i], recv_sem.at[0, i], far))
        beside.append(remote(source, slot, send_sem.at[1, i], recv_sem.at[1, i], near))
        across[-1].start()
        beside[-1].start()
    out_ref[mine, tensor_me] = in_ref[...]
    for i in range(2):
        across[i].wait()
        slot = out_ref.at[theirs, tensor_me, pl.ds(i * rows, rows)]
        passed.append(remote(slot, slot, send_sem.at[2, i], recv_sem.at[2, i], near))
        passed[-1].start()
    for copy in beside + passed:
        copy.wait()


def gather_rows(values, collective_id):
    out = pl.pallas_call(
        gather_rows_kernel,
        out_shape=jax.ShapeDtypeStruct((2, 2) + values.shape, values.dtype),
        in_specs=[pl.BlockSpec(memory_space=pltpu.VMEM)],
        out_specs=pl.BlockSpec(memory_space=pltpu.VMEM),
        scratch_shapes=[pltpu.SemaphoreType.DMA((3, 2))] * 2,
        compiler_params=pltpu.CompilerParams(collective_id=collective_id, has_side_effects=True),
    )(values)
    return out.reshape(-1, values.shape[-1])


def scatter_rows_kernel(count, *refs):
    refs = list(refs)
    ins = [refs.pop(0) for _ in range(count)]
    outs = [refs.pop(0) for _ in range(count)]
    landed = [refs.pop(0) for _ in range(count)]
    sent = [refs.pop(0) for _ in range(count)]
    got = [refs.pop(0) for _ in range(count)]
    send_sem, recv_sem = refs
    mine, theirs, tensor_me, near, far = group_place()
    group_barrier(near, far)
    parts = 2
    rows = outs[0].shape[0] // parts
    first, second, across = [], [], []

    def span(part):
        return pl.ds(part * rows, rows)

    for i in range(count):
        for part in range(parts):
            copy = remote(
                ins[i].at[theirs, 1 - tensor_me, span(part)],
                landed[i].at[0, span(part)],
                send_sem.at[i, 0, part],
                recv_sem.at[i, 0, part],
                near,
            )
            copy.start()
            first.append(copy)
        copy = remote(
            ins[i].at[mine, 1 - tensor_me],
            landed[i].at[1],
            send_sem.at[i, 1, 0],
            recv_sem.at[i, 1, 0],
            near,
        )
        copy.start()
        second.append(copy)
    for i in range(count):
        for part in range(parts):
            first[i * parts + part].wait_recv()

            def body(r, carry):
                at = pl.ds(pl.multiple_of(part * rows + r * 16, 16), 16)
                total = ins[i][theirs, tensor_me, at, :] + landed[i][0, at, :]
                sent[i][at, :] = total.astype(jnp.bfloat16)
                return carry

            lax.fori_loop(0, rows // 16, body, 0)
            copy = remote(
                sent[i].at[span(part)],
                got[i].at[span(part)],
                send_sem.at[i, 2, part],
                recv_sem.at[i, 2, part],
                far,
            )
            copy.start()
            across.append(copy)
    for i in range(count):
        second[i].wait_recv()
        for part in range(parts):
            across[i * parts + part].wait_recv()

            def body(r, carry):
                at = pl.ds(pl.multiple_of(part * rows + r * 16, 16), 16)
                total = ins[i][mine, tensor_me, at, :] + landed[i][1, at, :]
                outs[i][at, :] = total + got[i][at, :].astype(jnp.float32)
                return carry

            lax.fori_loop(0, rows // 16, body, 0)
    for copy in first + second + across:
        copy.wait_send()


def scatter_rows(partials, collective_id):
    count = len(partials)
    rows, width = partials[0].shape[0] // 4, partials[0].shape[1]
    whole = pl.BlockSpec(memory_space=pltpu.VMEM)
    return pl.pallas_call(
        functools.partial(scatter_rows_kernel, count),
        out_shape=[jax.ShapeDtypeStruct((rows, width), jnp.float32)] * count,
        in_specs=[whole] * count,
        out_specs=[whole] * count,
        scratch_shapes=[pltpu.VMEM((2, rows, width), jnp.float32)] * count
        + [pltpu.VMEM((rows, width), jnp.bfloat16)] * (2 * count)
        + [pltpu.SemaphoreType.DMA((count, 3, 2))] * 2,
        compiler_params=pltpu.CompilerParams(
            collective_id=collective_id, has_side_effects=True, vmem_limit_bytes=VMEM_LIMIT
        ),
    )(*[p.reshape(2, 2, rows, width) for p in partials])


def masked_scores(query_rot, key_rot, allowed, scaling):
    scores = (
        jnp.einsum("sqgrd,skgd->sgrqk", query_rot, key_rot, preferred_element_type=jnp.float32)
        * scaling
    )
    return jnp.where(allowed[:, None, None], scores, -1e30)


def per_device(
    tokens,
    cotangent,
    lengths,
    w_query,
    key_matrix,
    value_matrix,
    w_out,
    w_gate,
    w_up,
    w_down,
    gain_attn,
    gain_mlp,
    gain_query,
    gain_key,
):
    own_rows = tokens.shape[0]
    total_rows = own_rows * 2
    weights = (w_query, key_matrix, value_matrix, w_out, w_gate, w_up, w_down)
    halves = [w.shape[1] // 2 for w in weights]
    layouts = (
        ((0, halves[0]), (1, halves[1]), (2, halves[2])),
        ((3, halves[3]),),
        ((4, halves[4]), (5, halves[5])),
        ((6, halves[6]),),
    )
    own_index = lax.axis_index("tensor") * own_rows + jnp.arange(own_rows, dtype=jnp.int32)
    own_live = own_index < lengths[0]
    cot_live = jnp.where(own_live[:, None], cotangent, jnp.zeros_like(cotangent))
    scaling = HEAD_SIZE ** (-0.5)
    group_ratio = QUERY_HEADS // KEY_VALUE_HEADS
    token_values = tokens.astype(jnp.float32)
    attn_norm, attn_inverse = rms_rows(token_values, gain_attn)
    length_row = jnp.broadcast_to(lengths.astype(jnp.float32)[:, None], (8, HEAD_SIZE))
    fetched, row_sets, length_pair = gather_all(
        weights, layouts, (attn_norm.astype(jnp.bfloat16), cot_live), length_row, 0
    )
    full_qkv, full_out, full_gu, full_down = fetched
    normed, grad_result = row_sets
    positions, allowed = jax.vmap(lambda n: layout(n, total_rows))(length_pair.astype(jnp.int32))
    cosine, sine_part = rope_tables(positions.reshape(-1), HEAD_SIZE)
    cosine, sine_part = (t.reshape(2, total_rows, -1) for t in (cosine, sine_part))
    cos_query, sin_query = (cosine[:, :, None, None, :], sine_part[:, :, None, None, :])
    cos_key, sin_key = (cosine[:, :, None, :], sine_part[:, :, None, :])
    kv_heads = halves[1] // HEAD_SIZE
    q_end, k_end = halves[0], halves[0] + halves[1]
    qkv = jnp.dot(normed, full_qkv, preferred_element_type=jnp.float32)
    query_raw = qkv[:, :q_end].reshape(2, total_rows, kv_heads, group_ratio, HEAD_SIZE)
    key_raw = qkv[:, q_end:k_end].reshape(2, total_rows, kv_heads, HEAD_SIZE)
    value_part = qkv[:, k_end:].astype(jnp.bfloat16).reshape(2, total_rows, kv_heads, HEAD_SIZE)
    query_normed, query_inverse = rms_rows(query_raw, gain_query)
    key_normed, key_inverse = rms_rows(key_raw, gain_key)
    query_rot = rotate(query_normed, cos_query, sin_query).astype(jnp.bfloat16)
    key_rot = rotate(key_normed, cos_key, sin_key).astype(jnp.bfloat16)
    scores = masked_scores(query_rot, key_rot, allowed, scaling)
    row_max = jnp.max(scores, axis=-1, keepdims=True)
    log_total = row_max + jnp.log(jnp.sum(jnp.exp(scores - row_max), axis=-1, keepdims=True))
    attn_probs = jnp.exp(scores - log_total).astype(jnp.bfloat16)
    mixed = jnp.einsum(
        "sgrqk,skgd->sqgrd", attn_probs, value_part, preferred_element_type=jnp.float32
    ).astype(jnp.bfloat16)
    mixed_flat = mixed.reshape(2 * total_rows, -1)
    resid = token_values + scatter_rows([product_t(mixed_flat, full_out)], 7)[0]
    mlp_norm, mlp_inverse = rms_rows(resid, gain_mlp)
    mlp_in = gather_rows(mlp_norm.astype(jnp.bfloat16), 4)
    gate_up = jnp.dot(mlp_in, full_gu, preferred_element_type=jnp.float32)
    gate_proj, up_proj = gate_up[:, : halves[4]], gate_up[:, halves[4] :]
    activation = (jax.nn.silu(gate_proj) * up_proj).astype(jnp.bfloat16)
    grad_act = jnp.dot(grad_result, full_down, preferred_element_type=jnp.float32)
    sigma = jax.nn.sigmoid(gate_proj)
    grad_gate = (grad_act * up_proj * sigma * (1.0 + gate_proj * (1.0 - sigma))).astype(
        jnp.bfloat16
    )
    grad_up = (grad_act * gate_proj * sigma).astype(jnp.bfloat16)
    grad_gu = jnp.concatenate([grad_gate, grad_up], axis=1)
    grad_mlp_in, down_rows = scatter_rows(
        [product_t(grad_gu, full_gu), product_t(activation, full_down)], 8
    )
    result = (resid + down_rows).astype(jnp.bfloat16)
    grad_w_down = product_tn(grad_result, activation)
    grad_w_gu = product_tn(mlp_in, grad_gu)
    grad_resid_mlp, grad_gain_mlp = rms_back(grad_mlp_in, resid, mlp_inverse, gain_mlp)
    grad_resid = cot_live.astype(jnp.float32) + grad_resid_mlp
    grad_attn = gather_rows(grad_resid.astype(jnp.bfloat16), 6)
    grad_w_out = product_tn(grad_attn, mixed_flat)
    grad_mixed = (
        jnp.dot(grad_attn, full_out, preferred_element_type=jnp.float32)
        .astype(jnp.bfloat16)
        .reshape(2, total_rows, kv_heads, group_ratio, HEAD_SIZE)
    )
    scores = masked_scores(query_rot, key_rot, allowed, scaling)
    probs_full = jnp.exp(scores - log_total)
    probs_half = probs_full.astype(jnp.bfloat16)
    grad_value = jnp.einsum(
        "sgrqk,sqgrd->skgd", probs_half, grad_mixed, preferred_element_type=jnp.float32
    )
    grad_probs = jnp.einsum(
        "sqgrd,skgd->sgrqk", grad_mixed, value_part, preferred_element_type=jnp.float32
    )
    row_delta = jnp.sum(grad_mixed.astype(jnp.float32) * mixed.astype(jnp.float32), axis=-1)
    row_delta = jnp.transpose(row_delta, (0, 2, 3, 1))[..., None]
    grad_scores = (probs_full * (grad_probs - row_delta) * scaling).astype(jnp.bfloat16)
    grad_query_rot = jnp.einsum(
        "sgrqk,skgd->sqgrd", grad_scores, key_rot, preferred_element_type=jnp.float32
    )
    grad_key_rot = jnp.einsum(
        "sgrqk,sqgrd->skgd", grad_scores, query_rot, preferred_element_type=jnp.float32
    )
    grad_query_raw, grad_gain_query = rms_back(
        rotate_back(grad_query_rot, cos_query, sin_query), query_raw, query_inverse, gain_query
    )
    grad_key_raw, grad_gain_key = rms_back(
        rotate_back(grad_key_rot, cos_key, sin_key), key_raw, key_inverse, gain_key
    )
    grad_qkv = jnp.concatenate(
        [
            part.astype(jnp.bfloat16).reshape(2 * total_rows, -1)
            for part in (grad_query_raw, grad_key_raw, grad_value)
        ],
        axis=1,
    )
    grad_w_qkv = product_tn(normed, grad_qkv)
    grad_normed = scatter_rows([product_t(grad_qkv, full_qkv)], 10)[0]
    grad_tokens_attn, grad_gain_attn = rms_back(grad_normed, token_values, attn_inverse, gain_attn)
    grad_tokens = grad_resid + grad_tokens_attn
    gain_parts = (grad_gain_attn, grad_gain_mlp, grad_gain_query, grad_gain_key)
    gain_rows = [part.reshape(-1, HEAD_SIZE) for part in gain_parts]
    used = sum(part.shape[0] for part in gain_rows)
    gain_rows.append(jnp.zeros((-used % 8, HEAD_SIZE), jnp.float32))
    weight_sums, gain_sum = reduce_weights(
        [g.astype(jnp.bfloat16) for g in (grad_w_qkv, grad_w_out, grad_w_gu, grad_w_down)],
        layouts,
        [w.shape[1] for w in weights],
        jnp.concatenate(gain_rows, axis=0),
        collective_id=1,
    )
    gain_totals, row = [], 0
    for part in gain_parts:
        taken = part.shape[0] // HEAD_SIZE
        gain_totals.append(gain_sum[row : row + taken].reshape(-1))
        row += taken
    return (result, grad_tokens, *weight_sums, *gain_totals)


def solution(mesh):
    in_specs = (
        P(("dp", "tensor"), None),
        P(("dp", "tensor"), None),
        P("dp"),
        P("dp", "tensor"),
        P("dp", "tensor"),
        P("dp", "tensor"),
        P("dp", "tensor"),
        P("dp", "tensor"),
        P("dp", "tensor"),
        P("dp", "tensor"),
        P(),
        P(),
        P(),
        P(),
    )
    out_specs = (
        P(("dp", "tensor"), None),
        P(("dp", "tensor"), None),
        P("dp", "tensor"),
        P("dp", "tensor"),
        P("dp", "tensor"),
        P("dp", "tensor"),
        P("dp", "tensor"),
        P("dp", "tensor"),
        P("dp", "tensor"),
        P(),
        P(),
        P(),
        P(),
    )
    return jax.shard_map(
        per_device, mesh=mesh, in_specs=in_specs, out_specs=out_specs, check_vma=False
    )
```

```python
import functools
import math

import jax
import jax.numpy as jnp
from jax import lax
from jax.experimental import pallas as pl
from jax.experimental.pallas import tpu as pltpu
from jax.sharding import PartitionSpec as P

MESH = pl.DeviceIdType.MESH
VMEM_LIMIT = 64000000

HEAD_SIZE = 128


norm_eps = 1e-06
rope_base = 1000000.0


def rms_rows(values, gain_vec):
    inverse = lax.rsqrt(jnp.mean(values * values, axis=-1, keepdims=True) + norm_eps)
    return (values * inverse * gain_vec, inverse)


def rms_back(grad_output, values, inverse, gain_vec):
    scaled = grad_output * gain_vec
    mean_term = jnp.mean(scaled * values, axis=-1, keepdims=True)
    grad_values = inverse * scaled - values * (inverse * inverse * inverse) * mean_term
    flat_terms = (grad_output * values * inverse).reshape(-1, values.shape[-1])
    return (grad_values, jnp.sum(flat_terms, axis=0))


def rope_tables(positions, head_width):
    half_width = head_width // 2
    frequency = jnp.exp(
        -jnp.log(rope_base) * (2.0 * jnp.arange(half_width, dtype=jnp.float32) / head_width)
    )
    angles = positions.astype(jnp.float32)[:, None] * frequency[None, :]
    return (jnp.cos(angles), jnp.sin(angles))


def product_t(left, right):
    return lax.dot_general(
        left, right, (((1,), (1,)), ((), ())), preferred_element_type=jnp.float32
    )


def product_tn(left, right):
    return lax.dot_general(
        left, right, (((0,), (0,)), ((), ())), preferred_element_type=jnp.float32
    )


def split_dims(count):
    return (count // 8, 2, 2, 2)


PAIR = 1
AHEAD = 5
DEPTH = 2
RUN = 3
LAG = 2
INNER = ((0, 2, 3), (0, 3, 2))


def pieces(layouts):
    chunks = []
    for out_index, members in enumerate(layouts):
        column = 0
        for index, half in members:
            step = math.gcd(half, 256)
            parts = half // step
            for part in range(parts):
                order = INNER[len(chunks) % len(INNER)]
                chunks.append((index, part * step, step, out_index, column + part * step, order))
            column += half
    return chunks


class Place:
    def __init__(self, sizes):
        self.sizes = sizes
        self.me = lax.axis_index("dp")
        self.strides = [math.prod(sizes[i + 1 :]) for i in range(len(sizes))]
        self.coords = [
            lax.rem(lax.div(self.me, stride), size) for stride, size in zip(self.strides, sizes)
        ]
        self.base = [sum(size - 1 for size in sizes[:i]) for i in range(len(sizes))]

    def other(self, dim, offset):
        return lax.rem(self.coords[dim] + offset, self.sizes[dim])

    def peer(self, dim, offset):
        return self.me + (self.other(dim, offset) - self.coords[dim]) * self.strides[dim]

    def slot(self, dim, offset):
        return self.base[dim] + offset - 1

    def barrier(self, extra=()):
        barrier = pltpu.get_barrier_semaphore()
        count = 0
        for dim, size in enumerate(self.sizes):
            for offset in range(1, size):
                pl.semaphore_signal(
                    barrier, inc=1, device_id={"dp": self.peer(dim, offset)}, device_id_type=MESH
                )
                count += 1
        for target in extra:
            pl.semaphore_signal(barrier, inc=1, device_id=target, device_id_type=MESH)
            count += 1
        pl.semaphore_wait(barrier, count)


def remote(source, target, send, recv, device):
    return pltpu.make_async_remote_copy(
        src_ref=source,
        dst_ref=target,
        send_sem=send,
        recv_sem=recv,
        device_id=device,
        device_id_type=MESH,
    )


def gather_kernel(sizes, chunks, counts, *refs):
    n_in, n_out, n_rows = counts
    refs = list(refs)
    ins = [refs.pop(0) for _ in range(n_in)]
    row_ins = [refs.pop(0) for _ in range(n_rows)]
    length_in = refs.pop(0)
    outs = [refs.pop(0) for _ in range(n_out)]
    row_outs = [refs.pop(0) for _ in range(n_rows)]
    length_out = refs.pop(0)
    send_sem, recv_sem, local_sem, row_send, row_recv, length_sem = refs
    place = Place(sizes)
    k = len(sizes)
    mine = place.coords[PAIR]
    theirs = place.other(PAIR, 1)
    tensor_me = lax.axis_index("tensor")
    near = {"tensor": 1 - tensor_me}
    far = {"dp": place.peer(PAIR, 1)}

    def region(chunk, done, dim=None, coord=None):
        where = []
        for i in range(k):
            if i == dim:
                where.append(coord)
            elif i in done:
                where.append(slice(None))
            else:
                where.append(place.coords[i])
        return outs[chunk[3]].at[tuple(where) + (slice(None), pl.ds(chunk[4], chunk[2]))]

    def source_of(chunk, half_index):
        half = ins[chunk[0]].shape[1] // 2
        start = pl.multiple_of(half_index * half + chunk[1], 128)
        return ins[chunk[0]].at[:, pl.ds(start, chunk[2])]

    def steps(chunk):
        return (PAIR,) + chunk[5]

    def sends(j, stage):
        chunk = chunks[j]
        order = steps(chunk)
        dim, done = order[stage], order[:stage]
        block = region(chunk, done)
        source = source_of(chunk, theirs) if stage == 0 else block
        return [
            remote(
                source,
                block,
                send_sem.at[j, place.slot(dim, offset)],
                recv_sem.at[j, place.slot(dim, offset)],
                {"dp": place.peer(dim, offset)},
            )
            for offset in range(1, sizes[dim])
        ]

    def wait_arrivals(j, stage):
        chunk = chunks[j]
        order = steps(chunk)
        dim, done = order[stage], order[:stage]
        for offset in range(1, sizes[dim]):
            block = region(chunk, done, dim, place.other(dim, sizes[dim] - offset))
            remote(
                block,
                block,
                send_sem.at[j, place.slot(dim, offset)],
                recv_sem.at[j, place.slot(dim, offset)],
                {"dp": place.peer(dim, offset)},
            ).wait_recv()

    place.barrier([near])
    started, own = [], []
    crossing = remote(
        length_in, length_out.at[mine], length_sem.at[0], length_sem.at[1], far
    )
    crossing.start()
    rows_far, rows_near, passed = [], [], []

    def send_rows(i):
        slot = row_outs[i].at[mine, tensor_me]
        rows_far.append(remote(row_ins[i], slot, row_send.at[i, 0], row_recv.at[i, 0], far))
        rows_near.append(remote(row_ins[i], slot, row_send.at[i, 1], row_recv.at[i, 1], near))
        rows_far[-1].start()
        rows_near[-1].start()
        row_outs[i][mine, tensor_me] = row_ins[i][...]

    def pass_rows(i):
        rows_far[i].wait()
        slot = row_outs[i].at[theirs, tensor_me]
        passed.append(remote(slot, slot, row_send.at[i, 2], row_recv.at[i, 2], near))
        passed[-1].start()

    def begin(j):
        copies = sends(j, 0)
        for copy in copies:
            copy.start()
        started.extend(copies)
        copy = pltpu.make_async_copy(
            source_of(chunks[j], mine), region(chunks[j], ()), local_sem.at[j]
        )
        copy.start()
        own.append(copy)

    for j in range(min(AHEAD, len(chunks))):
        begin(j)
    length_out[mine] = length_in[...]
    total_steps = len(chunks) + DEPTH * (k - 1)
    for step in range(total_steps):
        if step + AHEAD < len(chunks):
            begin(step + AHEAD)
        for i in range(n_rows):
            if step == min(4 + 3 * i, total_steps - 1):
                send_rows(i)
        for stage in range(k, 0, -1):
            j = step - DEPTH * (stage - 1)
            if not 0 <= j < len(chunks):
                continue
            if stage == 1:
                own[j].wait()
            wait_arrivals(j, stage - 1)
            if stage < k:
                copies = sends(j, stage)
                for copy in copies:
                    copy.start()
                started += copies
        for i in range(n_rows):
            if step == min(12 + i, total_steps - 1):
                pass_rows(i)
    crossing.wait()
    for copy in rows_near + passed:
        copy.wait()
    for copy in started:
        copy.wait_send()


def gather_all(weights, layouts, rows, length_row, collective_id):
    sizes = split_dims(lax.axis_size("dp"))
    chunks = pieces(layouts)
    peers = sum(size - 1 for size in sizes)
    n_in, n_out, n_rows = len(weights), len(layouts), len(rows)
    depth = weights[0].shape[0]
    whole = pl.BlockSpec(memory_space=pltpu.VMEM)
    outs = pl.pallas_call(
        functools.partial(gather_kernel, sizes, chunks, (n_in, n_out, n_rows)),
        out_shape=[
            jax.ShapeDtypeStruct(sizes + (depth, sum(half for _, half in members)), jnp.bfloat16)
            for members in layouts
        ]
        + [jax.ShapeDtypeStruct((2, 2) + r.shape, r.dtype) for r in rows]
        + [jax.ShapeDtypeStruct((2,) + length_row.shape, length_row.dtype)],
        in_specs=[whole] * (n_in + n_rows + 1),
        out_specs=[pl.BlockSpec(memory_space=pl.ANY)] * n_out + [whole] * (n_rows + 1),
        scratch_shapes=[
            pltpu.SemaphoreType.DMA((len(chunks), peers)),
            pltpu.SemaphoreType.DMA((len(chunks), peers)),
            pltpu.SemaphoreType.DMA((len(chunks),)),
            pltpu.SemaphoreType.DMA((n_rows, 3)),
            pltpu.SemaphoreType.DMA((n_rows, 3)),
            pltpu.SemaphoreType.DMA((2,)),
        ],
        compiler_params=pltpu.CompilerParams(
            collective_id=collective_id, has_side_effects=True, vmem_limit_bytes=VMEM_LIMIT
        ),
    )(*weights, *rows, length_row)
    full = [out.reshape(-1, out.shape[-1]) for out in outs[:n_out]]
    row_sets = [out.reshape(-1, out.shape[-1]) for out in outs[n_out : n_out + n_rows]]
    return full, row_sets, outs[n_out + n_rows][:, 0, 0]


def reduce_kernel(sizes, chunks, counts, tensor_size, *refs):
    n_in, n_out = counts
    refs = list(refs)
    ins = [refs.pop(0) for _ in range(n_in)]
    gains = refs.pop(0)
    outs = [refs.pop(0) for _ in range(n_out)]
    gain_out = refs.pop(0)
    k = len(sizes)
    m = k - 1
    held = [[refs.pop(0) for _ in range(m - 1)] for _ in chunks]
    landed = [[refs.pop(0) for _ in range(m)] for _ in chunks]
    crossed = [refs.pop(0) for _ in chunks]
    gain_held = [refs.pop(0) for _ in range(k)]
    gain_landed = [refs.pop(0) for _ in range(k + 1)]
    send_sem, recv_sem, local_sem, gain_send, gain_recv = refs
    place = Place(sizes)
    tensor_me = lax.axis_index("tensor")
    mine = place.coords[PAIR]
    theirs = place.other(PAIR, 1)
    rows = ins[0].shape[-2]

    def order_of(j):
        return tuple(reversed(chunks[j][5]))

    def part(ref, dims, dim, coord, columns):
        where = tuple(coord if i == dim else slice(None) for i in dims)
        return ref.at[where + (slice(None), columns)]

    def copies_of(j, stage):
        _, _, width, array, column, _ = chunks[j]
        order = order_of(j)
        dim = order[stage]
        dims = [i for i in range(k) if i not in order[:stage]]
        if stage == 0:
            ref, columns = ins[array], pl.ds(column, width)
        else:
            ref, columns = held[j][stage - 1], slice(None)
        return [
            remote(
                part(ref, dims, dim, place.other(dim, offset), columns),
                landed[j][stage].at[offset - 1],
                send_sem.at[j, place.slot(dim, offset)],
                recv_sem.at[j, place.slot(dim, offset)],
                {"dp": place.peer(dim, offset)},
            )
            for offset in range(1, sizes[dim])
        ]

    def result_at(j):
        index, start, width = chunks[j][:3]
        half = outs[index].shape[1] // 2
        return outs[index], pl.ds(pl.multiple_of(mine * half + start, 128), width)

    def cross_copy(j):
        out, columns = result_at(j)
        slot = place.slot(PAIR, 1)
        return remote(
            crossed[j],
            out.at[:, columns],
            send_sem.at[j, slot],
            recv_sem.at[j, slot],
            {"dp": place.peer(PAIR, 1)},
        )

    def add_up(j, stage):
        order = order_of(j)
        dim = order[stage]
        dims = [i for i in range(k) if i not in order[:stage]]
        lead = [sizes[i] for i in dims if i != dim]
        per = rows // 16

        def total_of(where, rows_at):
            if stage == 0:
                own = tuple(where)
                source = held[j][0]
            else:
                own = list(where)
                own.insert(dims.index(dim), place.coords[dim])
                own = tuple(own)
                source = held[j][stage - 1]
            total = source[own + (rows_at, slice(None))].astype(jnp.float32)
            for offset in range(1, sizes[dim]):
                got = landed[j][stage][(offset - 1,) + tuple(where) + (rows_at, slice(None))]
                total = total + got.astype(jnp.float32)
            return total

        if stage == m - 1:

            def last(i, carry):
                rows_at = pl.ds(pl.multiple_of(i * 16, 16), 16)
                crossed[j][rows_at, :] = total_of((theirs,), rows_at)
                return carry

            lax.fori_loop(0, per, last, 0)
            copy = cross_copy(j)
            copy.start()

            def keep(i, carry):
                rows_at = pl.ds(pl.multiple_of(i * 16, 16), 16)
                out, columns = result_at(j)
                out[rows_at, columns] = total_of((mine,), rows_at)
                return carry

            lax.fori_loop(0, per, keep, 0)
            return copy

        def body(i, carry):
            rows_at = pl.ds(pl.multiple_of(lax.rem(i, per) * 16, 16), 16)
            flat = lax.div(i, per)
            where = []
            for position in range(len(lead)):
                below = math.prod(lead[position + 1 :])
                where.append(lax.rem(lax.div(flat, below), lead[position]))
            total = total_of(where, rows_at)
            held[j][stage][tuple(where) + (rows_at, slice(None))] = total.astype(jnp.bfloat16)
            return carry

        lax.fori_loop(0, math.prod(lead) * per, body, 0)
        return None

    def gain_copies(stage):
        source = gains if stage == 0 else gain_held[stage - 1]
        result = []
        if stage < k:
            for offset in range(1, sizes[stage]):
                slot = place.slot(stage, offset)
                result.append(
                    remote(
                        source,
                        gain_landed[stage].at[offset - 1],
                        gain_send.at[slot],
                        gain_recv.at[slot],
                        {"dp": place.peer(stage, offset)},
                    )
                )
        else:
            first = sum(size - 1 for size in sizes)
            for offset in range(1, tensor_size):
                result.append(
                    remote(
                        source,
                        gain_landed[stage].at[offset - 1],
                        gain_send.at[first + offset - 1],
                        gain_recv.at[first + offset - 1],
                        {"tensor": lax.rem(tensor_me + offset, tensor_size)},
                    )
                )
        return result

    place.barrier(
        [{"tensor": lax.rem(tensor_me + i, tensor_size)} for i in range(1, tensor_size)]
    )
    flights, own, crossing = [], [], []

    def begin(j):
        _, _, width, array, column, _ = chunks[j]
        first = copies_of(j, 0)
        for copy in first:
            copy.start()
        flights.append([first])
        dim = order_of(j)[0]
        copy = pltpu.make_async_copy(
            part(ins[array], range(k), dim, place.coords[dim], pl.ds(column, width)),
            held[j][0],
            local_sem.at[j],
        )
        copy.start()
        own.append(copy)

    for j in range(min(RUN, len(chunks))):
        begin(j)
    gain_flight = gain_copies(0)
    for copy in gain_flight:
        copy.start()
    for step in range(len(chunks) + LAG * (m - 1)):
        if step + RUN < len(chunks):
            begin(step + RUN)
        if step % 2 == 1 and step // 2 <= k:
            turn = step // 2
            for copy in gain_flight:
                copy.wait()
            total = (gains if turn == 0 else gain_held[turn - 1])[...]
            for i in range(len(gain_flight)):
                total = total + gain_landed[turn][i]
            if turn < k:
                gain_held[turn][...] = total
                gain_flight = gain_copies(turn + 1)
                for copy in gain_flight:
                    copy.start()
            else:
                gain_out[...] = total
        for stage in range(m - 1, -1, -1):
            j = step - LAG * stage
            if not 0 <= j < len(chunks):
                continue
            if stage == 0:
                own[j].wait()
            for copy in flights[j][stage]:
                copy.wait_recv()
            copy = add_up(j, stage)
            if stage < m - 1:
                following = copies_of(j, stage + 1)
                for copy in following:
                    copy.start()
                flights[j].append(following)
            else:
                crossing.append(copy)
    for copy in crossing:
        copy.wait_recv()
    for flight in flights:
        for copies in flight:
            for copy in copies:
                copy.wait_send()
    for copy in crossing:
        copy.wait_send()


def reduce_weights(grads, layouts, widths, gains, collective_id):
    sizes = split_dims(lax.axis_size("dp"))
    tensor_size = lax.axis_size("tensor")
    k = len(sizes)
    m = k - 1
    rows = grads[0].shape[0] // math.prod(sizes)
    chunks = pieces(layouts)
    peers = sum(size - 1 for size in sizes)
    n_in, n_out = len(grads), len(widths)
    held, landed, crossed = [], [], []
    for _, _, width, _, _, gather_order in chunks:
        order = tuple(reversed(gather_order))
        for stage in range(m):
            left = tuple(sizes[i] for i in range(k) if i not in order[: stage + 1])
            if stage < m - 1:
                held.append(pltpu.VMEM(left + (rows, width), jnp.bfloat16))
            landed.append(pltpu.VMEM((sizes[order[stage]] - 1,) + left + (rows, width), jnp.bfloat16))
        crossed.append(pltpu.VMEM((rows, width), jnp.float32))
    gain_landed = [pltpu.VMEM((size - 1,) + gains.shape, jnp.float32) for size in sizes + (tensor_size,)]
    whole = pl.BlockSpec(memory_space=pltpu.VMEM)
    outs = pl.pallas_call(
        functools.partial(reduce_kernel, sizes, chunks, (n_in, n_out), tensor_size),
        out_shape=[jax.ShapeDtypeStruct((rows, width), jnp.float32) for width in widths]
        + [jax.ShapeDtypeStruct(gains.shape, jnp.float32)],
        in_specs=[pl.BlockSpec(memory_space=pl.ANY)] * n_in + [whole],
        out_specs=[whole] * (n_out + 1),
        scratch_shapes=held
        + landed
        + crossed
        + [pltpu.VMEM(gains.shape, jnp.float32)] * k
        + gain_landed
        + [
            pltpu.SemaphoreType.DMA((len(chunks), peers)),
            pltpu.SemaphoreType.DMA((len(chunks), peers)),
            pltpu.SemaphoreType.DMA((len(chunks),)),
            pltpu.SemaphoreType.DMA((peers + tensor_size - 1,)),
            pltpu.SemaphoreType.DMA((peers + tensor_size - 1,)),
        ],
        compiler_params=pltpu.CompilerParams(
            collective_id=collective_id, has_side_effects=True, vmem_limit_bytes=VMEM_LIMIT
        ),
    )(*[g.reshape(sizes + (rows, g.shape[1])) for g in grads], gains)
    return outs[:n_out], outs[n_out]


def group_place():
    sizes = split_dims(lax.axis_size("dp"))
    place = Place(sizes)
    tensor_me = lax.axis_index("tensor")
    near = {"tensor": 1 - tensor_me}
    far = {"dp": place.peer(PAIR, 1)}
    return place.coords[PAIR], place.other(PAIR, 1), tensor_me, near, far


def group_barrier(near, far):
    barrier = pltpu.get_barrier_semaphore()
    pl.semaphore_signal(barrier, inc=1, device_id=near, device_id_type=MESH)
    pl.semaphore_signal(barrier, inc=1, device_id=far, device_id_type=MESH)
    pl.semaphore_wait(barrier, 2)


def gather_rows_kernel(in_ref, out_ref, send_sem, recv_sem):
    mine, theirs, tensor_me, near, far = group_place()
    group_barrier(near, far)
    rows = in_ref.shape[0] // 2
    across, beside, passed = [], [], []
    for i in range(2):
        source = in_ref.at[pl.ds(i * rows, rows)]
        slot = out_ref.at[mine, tensor_me, pl.ds(i * rows, rows)]
        across.append(remote(source, slot, send_sem.at[0, i], recv_sem.at[0, i], far))
        beside.append(remote(source, slot, send_sem.at[1, i], recv_sem.at[1, i], near))
        across[-1].start()
        beside[-1].start()
    out_ref[mine, tensor_me] = in_ref[...]
    for i in range(2):
        across[i].wait()
        slot = out_ref.at[theirs, tensor_me, pl.ds(i * rows, rows)]
        passed.append(remote(slot, slot, send_sem.at[2, i], recv_sem.at[2, i], near))
        passed[-1].start()
    for copy in beside + passed:
        copy.wait()


def gather_rows(values, collective_id):
    out = pl.pallas_call(
        gather_rows_kernel,
        out_shape=jax.ShapeDtypeStruct((2, 2) + values.shape, values.dtype),
        in_specs=[pl.BlockSpec(memory_space=pltpu.VMEM)],
        out_specs=pl.BlockSpec(memory_space=pltpu.VMEM),
        scratch_shapes=[pltpu.SemaphoreType.DMA((3, 2))] * 2,
        compiler_params=pltpu.CompilerParams(collective_id=collective_id, has_side_effects=True),
    )(values)
    return out.reshape(-1, values.shape[-1])


def scatter_rows_kernel(count, *refs):
    refs = list(refs)
    ins = [refs.pop(0) for _ in range(count)]
    outs = [refs.pop(0) for _ in range(count)]
    landed = [refs.pop(0) for _ in range(count)]
    sent = [refs.pop(0) for _ in range(count)]
    got = [refs.pop(0) for _ in range(count)]
    send_sem, recv_sem = refs
    mine, theirs, tensor_me, near, far = group_place()
    group_barrier(near, far)
    parts = 2
    rows = outs[0].shape[0] // parts
    first, second, across = [], [], []

    def span(part):
        return pl.ds(part * rows, rows)

    for i in range(count):
        for part in range(parts):
            copy = remote(
                ins[i].at[theirs, 1 - tensor_me, span(part)],
                landed[i].at[0, span(part)],
                send_sem.at[i, 0, part],
                recv_sem.at[i, 0, part],
                near,
            )
            copy.start()
            first.append(copy)
        copy = remote(
            ins[i].at[mine, 1 - tensor_me],
            landed[i].at[1],
            send_sem.at[i, 1, 0],
            recv_sem.at[i, 1, 0],
            near,
        )
        copy.start()
        second.append(copy)
    for i in range(count):
        for part in range(parts):
            first[i * parts + part].wait_recv()

            def body(r, carry):
                at = pl.ds(pl.multiple_of(part * rows + r * 16, 16), 16)
                total = ins[i][theirs, tensor_me, at, :] + landed[i][0, at, :]
                sent[i][at, :] = total.astype(jnp.bfloat16)
                return carry

            lax.fori_loop(0, rows // 16, body, 0)
            copy = remote(
                sent[i].at[span(part)],
                got[i].at[span(part)],
                send_sem.at[i, 2, part],
                recv_sem.at[i, 2, part],
                far,
            )
            copy.start()
            across.append(copy)
    for i in range(count):
        second[i].wait_recv()
        for part in range(parts):
            across[i * parts + part].wait_recv()

            def body(r, carry):
                at = pl.ds(pl.multiple_of(part * rows + r * 16, 16), 16)
                total = ins[i][mine, tensor_me, at, :] + landed[i][1, at, :]
                outs[i][at, :] = total + got[i][at, :].astype(jnp.float32)
                return carry

            lax.fori_loop(0, rows // 16, body, 0)
    for copy in first + second + across:
        copy.wait_send()


def scatter_rows(partials, collective_id):
    count = len(partials)
    rows, width = partials[0].shape[0] // 4, partials[0].shape[1]
    whole = pl.BlockSpec(memory_space=pltpu.VMEM)
    return pl.pallas_call(
        functools.partial(scatter_rows_kernel, count),
        out_shape=[jax.ShapeDtypeStruct((rows, width), jnp.float32)] * count,
        in_specs=[whole] * count,
        out_specs=[whole] * count,
        scratch_shapes=[pltpu.VMEM((2, rows, width), jnp.float32)] * count
        + [pltpu.VMEM((rows, width), jnp.bfloat16)] * (2 * count)
        + [pltpu.SemaphoreType.DMA((count, 3, 2))] * 2,
        compiler_params=pltpu.CompilerParams(
            collective_id=collective_id, has_side_effects=True, vmem_limit_bytes=VMEM_LIMIT
        ),
    )(*[p.reshape(2, 2, rows, width) for p in partials])


def turn(values, cosine, sine_part):
    return values * cosine + pltpu.roll(values, HEAD_SIZE // 2, 1) * sine_part


def dot_rows(left, right):
    return jnp.dot(left, right, preferred_element_type=jnp.float32)


def head_at(index):
    return slice(index * HEAD_SIZE, (index + 1) * HEAD_SIZE)


def attend_kernel(
    lengths, x, w, wo, gain_q, gain_k, cosine, sine_part,
    raw, rot, value, mixed, probs, out,
):
    length_rows = x.shape[0] // 2
    kv_heads = value.shape[1] // HEAD_SIZE
    ratio = mixed.shape[1] // value.shape[1]
    q_heads = kv_heads * ratio
    wide = 2 * HEAD_SIZE
    scaling = HEAD_SIZE ** (-0.5)
    row = lax.broadcasted_iota(jnp.int32, (length_rows, length_rows), 0)
    column = lax.broadcasted_iota(jnp.int32, (length_rows, length_rows), 1)
    for s in range(2):
        rows = slice(s * length_rows, (s + 1) * length_rows)
        x_rows = x[rows, :]
        for block in range(w.shape[1] // wide):
            at = slice(block * wide, (block + 1) * wide)
            projected = dot_rows(x_rows, w[:, at])
            if at.start < raw.shape[1]:
                raw[rows, at] = projected
            else:
                value[rows, at.start - raw.shape[1] : at.stop - raw.shape[1]] = projected.astype(
                    jnp.bfloat16
                )
        for head in range(q_heads + kv_heads):
            part = raw[rows, head_at(head)]
            gain = (gain_q if head < q_heads else gain_k)[...]
            normed, _ = rms_rows(part, gain)
            rot[rows, head_at(head)] = turn(normed, cosine[rows, :], sine_part[rows, :]).astype(
                jnp.bfloat16
            )
        live = (row < lengths[s]) & (column <= row)
        allowed = live | (row == column)
        for head in range(q_heads):
            group = head // ratio
            scores = product_t(rot[rows, head_at(head)], rot[rows, head_at(q_heads + group)])
            scores = jnp.where(allowed, scores * scaling, -1e30)
            row_max = jnp.max(scores, axis=-1, keepdims=True)
            total = jnp.sum(jnp.exp(scores - row_max), axis=-1, keepdims=True)
            shares = jnp.exp(scores - (row_max + jnp.log(total)))
            probs[s * q_heads + head] = shares
            mixed[rows, head_at(head)] = dot_rows(
                shares.astype(jnp.bfloat16), value[rows, head_at(group)]
            ).astype(jnp.bfloat16)
        for block in range(wo.shape[0] // wide):
            at = slice(block * wide, (block + 1) * wide)
            out[rows, at] = product_t(mixed[rows, :], wo[at, :])


def attend(lengths, normed, full_qkv, full_out, gain_query, gain_key, cosine, sine_part):
    rows = normed.shape[0]
    mixed_width = full_out.shape[1]
    value_width = (full_qkv.shape[1] - mixed_width) // 2
    raw_width = mixed_width + value_width
    count = 2 * (mixed_width // HEAD_SIZE)
    whole = pl.BlockSpec(memory_space=pltpu.VMEM)
    return pl.pallas_call(
        attend_kernel,
        out_shape=[
            jax.ShapeDtypeStruct((rows, raw_width), jnp.float32),
            jax.ShapeDtypeStruct((rows, raw_width), jnp.bfloat16),
            jax.ShapeDtypeStruct((rows, value_width), jnp.bfloat16),
            jax.ShapeDtypeStruct((rows, mixed_width), jnp.bfloat16),
            jax.ShapeDtypeStruct((count, rows // 2, rows // 2), jnp.float32),
            jax.ShapeDtypeStruct((rows, full_out.shape[0]), jnp.float32),
        ],
        in_specs=[pl.BlockSpec(memory_space=pltpu.SMEM)] + [whole] * 7,
        out_specs=[whole] * 6,
        compiler_params=pltpu.CompilerParams(vmem_limit_bytes=VMEM_LIMIT // 2),
    )(
        lengths, normed, full_qkv, full_out, gain_query[None], gain_key[None], cosine, sine_part
    )


def attend_back_kernel(
    grad, w, wo, gain_q, gain_k, cosine, sine_part, raw, rot, value, mixed, probs,
    grad_qkv, terms, gain_q_out, gain_k_out, grad_mixed,
):
    length_rows = grad.shape[0] // 2
    kv_heads = value.shape[1] // HEAD_SIZE
    ratio = mixed.shape[1] // value.shape[1]
    q_heads = kv_heads * ratio
    wide = 2 * HEAD_SIZE
    scaling = HEAD_SIZE ** (-0.5)
    gain_q_out[...] = jnp.zeros_like(gain_q_out)
    gain_k_out[...] = jnp.zeros_like(gain_k_out)
    for s in range(2):
        rows = slice(s * length_rows, (s + 1) * length_rows)

        def finish(grad_rot, head):
            gain, gain_out = (gain_q, gain_q_out) if head < q_heads else (gain_k, gain_k_out)
            upstream = turn(grad_rot, cosine[rows, :], -sine_part[rows, :])
            part = raw[rows, head_at(head)]
            _, inverse = rms_rows(part, gain[...])
            grad_raw, grad_gain = rms_back(upstream, part, inverse, gain[...])
            grad_qkv[rows, head_at(head)] = grad_raw.astype(jnp.bfloat16)
            gain_out[...] += grad_gain[None]

        grad_rows = grad[rows, :]
        for block in range(wo.shape[1] // wide):
            at = slice(block * wide, (block + 1) * wide)
            grad_mixed[:, at] = dot_rows(grad_rows, wo[:, at]).astype(jnp.bfloat16)
        for group in range(kv_heads):
            grad_key, grad_value = None, None
            for member in range(ratio):
                head = group * ratio + member
                shares = probs[s * q_heads + head]
                upstream = grad_mixed[:, head_at(head)]
                share_grads = product_t(upstream, value[rows, head_at(group)])
                delta = jnp.sum(
                    upstream.astype(jnp.float32)
                    * mixed[rows, head_at(head)].astype(jnp.float32),
                    axis=-1,
                    keepdims=True,
                )
                grad_scores = (shares * (share_grads - delta) * scaling).astype(jnp.bfloat16)
                to_value = product_tn(shares.astype(jnp.bfloat16), upstream)
                to_key = product_tn(grad_scores, rot[rows, head_at(head)])
                grad_value = to_value if grad_value is None else grad_value + to_value
                grad_key = to_key if grad_key is None else grad_key + to_key
                finish(dot_rows(grad_scores, rot[rows, head_at(q_heads + group)]), head)
            finish(grad_key, q_heads + group)
            grad_qkv[rows, head_at(q_heads + kv_heads + group)] = grad_value.astype(jnp.bfloat16)
        for block in range(w.shape[0] // wide):
            at = slice(block * wide, (block + 1) * wide)
            terms[rows, at] = product_t(grad_qkv[rows, :], w[at, :])


def attend_back(grad_attn, full_qkv, full_out, gain_query, gain_key, cosine, sine_part, saved):
    rows = grad_attn.shape[0]
    whole = pl.BlockSpec(memory_space=pltpu.VMEM)
    grad_qkv, terms, gain_q, gain_k = pl.pallas_call(
        attend_back_kernel,
        out_shape=[
            jax.ShapeDtypeStruct((rows, full_qkv.shape[1]), jnp.bfloat16),
            jax.ShapeDtypeStruct((rows, full_qkv.shape[0]), jnp.float32),
            jax.ShapeDtypeStruct((1, HEAD_SIZE), jnp.float32),
            jax.ShapeDtypeStruct((1, HEAD_SIZE), jnp.float32),
        ],
        in_specs=[whole] * 12,
        out_specs=[whole] * 4,
        scratch_shapes=[pltpu.VMEM((rows // 2, full_out.shape[1]), jnp.bfloat16)],
        compiler_params=pltpu.CompilerParams(vmem_limit_bytes=VMEM_LIMIT // 2),
    )(
        grad_attn, full_qkv, full_out, gain_query[None], gain_key[None], cosine, sine_part, *saved
    )
    return grad_qkv, terms, gain_q[0], gain_k[0]


def per_device(
    tokens,
    cotangent,
    lengths,
    w_query,
    key_matrix,
    value_matrix,
    w_out,
    w_gate,
    w_up,
    w_down,
    gain_attn,
    gain_mlp,
    gain_query,
    gain_key,
):
    own_rows = tokens.shape[0]
    total_rows = own_rows * 2
    weights = (w_query, key_matrix, value_matrix, w_out, w_gate, w_up, w_down)
    halves = [w.shape[1] // 2 for w in weights]
    layouts = (
        ((0, halves[0]), (1, halves[1]), (2, halves[2])),
        ((3, halves[3]),),
        ((4, halves[4]), (5, halves[5])),
        ((6, halves[6]),),
    )
    own_index = lax.axis_index("tensor") * own_rows + jnp.arange(own_rows, dtype=jnp.int32)
    own_live = own_index < lengths[0]
    cot_live = jnp.where(own_live[:, None], cotangent, jnp.zeros_like(cotangent))
    token_values = tokens.astype(jnp.float32)
    attn_norm, attn_inverse = rms_rows(token_values, gain_attn)
    length_row = jnp.broadcast_to(lengths.astype(jnp.float32)[:, None], (8, HEAD_SIZE))
    fetched, row_sets, length_pair = gather_all(
        weights, layouts, (attn_norm.astype(jnp.bfloat16), cot_live), length_row, 0
    )
    full_qkv, full_out, full_gu, full_down = fetched
    normed, grad_result = row_sets
    length_pair = length_pair.astype(jnp.int32)
    indices = jnp.arange(total_rows, dtype=jnp.int32)
    positions = jnp.where(indices[None] < length_pair[:, None], indices[None], 0).reshape(-1)
    cosine, sine_part = rope_tables(positions, HEAD_SIZE)
    cosine = jnp.concatenate([cosine, cosine], axis=1)
    sine_part = jnp.concatenate([-sine_part, sine_part], axis=1)
    qk_raw, rotated, value_part, mixed_flat, probs, mixed_terms = attend(
        length_pair, normed, full_qkv, full_out, gain_query, gain_key, cosine, sine_part
    )
    resid = token_values + scatter_rows([mixed_terms], 7)[0]
    mlp_norm, mlp_inverse = rms_rows(resid, gain_mlp)
    mlp_in = gather_rows(mlp_norm.astype(jnp.bfloat16), 4)
    gate_up = jnp.dot(mlp_in, full_gu, preferred_element_type=jnp.float32)
    gate_proj, up_proj = gate_up[:, : halves[4]], gate_up[:, halves[4] :]
    activation = (jax.nn.silu(gate_proj) * up_proj).astype(jnp.bfloat16)
    grad_act = jnp.dot(grad_result, full_down, preferred_element_type=jnp.float32)
    sigma = jax.nn.sigmoid(gate_proj)
    grad_gate = (grad_act * up_proj * sigma * (1.0 + gate_proj * (1.0 - sigma))).astype(
        jnp.bfloat16
    )
    grad_up = (grad_act * gate_proj * sigma).astype(jnp.bfloat16)
    grad_gu = jnp.concatenate([grad_gate, grad_up], axis=1)
    grad_mlp_in, down_rows = scatter_rows(
        [product_t(grad_gu, full_gu), product_t(activation, full_down)], 8
    )
    result = (resid + down_rows).astype(jnp.bfloat16)
    grad_w_down = product_tn(grad_result, activation)
    grad_w_gu = product_tn(mlp_in, grad_gu)
    grad_resid_mlp, grad_gain_mlp = rms_back(grad_mlp_in, resid, mlp_inverse, gain_mlp)
    grad_resid = cot_live.astype(jnp.float32) + grad_resid_mlp
    grad_attn = gather_rows(grad_resid.astype(jnp.bfloat16), 6)
    grad_w_out = product_tn(grad_attn, mixed_flat)
    saved = (qk_raw, rotated, value_part, mixed_flat, probs)
    grad_qkv, normed_terms, grad_gain_query, grad_gain_key = attend_back(
        grad_attn, full_qkv, full_out, gain_query, gain_key, cosine, sine_part, saved
    )
    grad_w_qkv = product_tn(normed, grad_qkv)
    grad_normed = scatter_rows([normed_terms], 10)[0]
    grad_tokens_attn, grad_gain_attn = rms_back(grad_normed, token_values, attn_inverse, gain_attn)
    grad_tokens = grad_resid + grad_tokens_attn
    gain_parts = (grad_gain_attn, grad_gain_mlp, grad_gain_query, grad_gain_key)
    gain_rows = [part.reshape(-1, HEAD_SIZE) for part in gain_parts]
    used = sum(part.shape[0] for part in gain_rows)
    gain_rows.append(jnp.zeros((-used % 8, HEAD_SIZE), jnp.float32))
    weight_sums, gain_sum = reduce_weights(
        [g.astype(jnp.bfloat16) for g in (grad_w_qkv, grad_w_out, grad_w_gu, grad_w_down)],
        layouts,
        [w.shape[1] for w in weights],
        jnp.concatenate(gain_rows, axis=0),
        collective_id=1,
    )
    gain_totals, row = [], 0
    for part in gain_parts:
        taken = part.shape[0] // HEAD_SIZE
        gain_totals.append(gain_sum[row : row + taken].reshape(-1))
        row += taken
    return (result, grad_tokens, *weight_sums, *gain_totals)


def solution(mesh):
    in_specs = (
        P(("dp", "tensor"), None),
        P(("dp", "tensor"), None),
        P("dp"),
        P("dp", "tensor"),
        P("dp", "tensor"),
        P("dp", "tensor"),
        P("dp", "tensor"),
        P("dp", "tensor"),
        P("dp", "tensor"),
        P("dp", "tensor"),
        P(),
        P(),
        P(),
        P(),
    )
    out_specs = (
        P(("dp", "tensor"), None),
        P(("dp", "tensor"), None),
        P("dp", "tensor"),
        P("dp", "tensor"),
        P("dp", "tensor"),
        P("dp", "tensor"),
        P("dp", "tensor"),
        P("dp", "tensor"),
        P("dp", "tensor"),
        P(),
        P(),
        P(),
        P(),
    )
    return jax.shard_map(
        per_device, mesh=mesh, in_specs=in_specs, out_specs=out_specs, check_vma=False
    )
```

```python
import functools
import math

import jax
import jax.numpy as jnp
from jax import lax
from jax.experimental import pallas as pl
from jax.experimental.pallas import tpu as pltpu
from jax.sharding import PartitionSpec as P

MESH = pl.DeviceIdType.MESH
VMEM_LIMIT = 64000000

HEAD_SIZE = 128


norm_eps = 1e-06
rope_base = 1000000.0


def rms_rows(values, gain_vec):
    inverse = lax.rsqrt(jnp.mean(values * values, axis=-1, keepdims=True) + norm_eps)
    return (values * inverse * gain_vec, inverse)


def rms_back(grad_output, values, inverse, gain_vec):
    scaled = grad_output * gain_vec
    mean_term = jnp.mean(scaled * values, axis=-1, keepdims=True)
    grad_values = inverse * scaled - values * (inverse * inverse * inverse) * mean_term
    flat_terms = (grad_output * values * inverse).reshape(-1, values.shape[-1])
    return (grad_values, jnp.sum(flat_terms, axis=0))


def rope_tables(positions, head_width):
    half_width = head_width // 2
    frequency = jnp.exp(
        -jnp.log(rope_base) * (2.0 * jnp.arange(half_width, dtype=jnp.float32) / head_width)
    )
    angles = positions.astype(jnp.float32)[:, None] * frequency[None, :]
    return (jnp.cos(angles), jnp.sin(angles))


def product_t(left, right):
    return lax.dot_general(
        left, right, (((1,), (1,)), ((), ())), preferred_element_type=jnp.float32
    )


def product_tn(left, right):
    return lax.dot_general(
        left, right, (((0,), (0,)), ((), ())), preferred_element_type=jnp.float32
    )


def split_dims(count):
    return (count // 8, 2, 2, 2)


PAIR = 1
PARTS = 4
AHEAD = 5
DEPTH = 2
RUN = 3
LAG = 2
INNER = ((0, 2, 3), (0, 3, 2))


def pieces(layouts):
    chunks = []
    for out_index, members in enumerate(layouts):
        column = 0
        for index, half in members:
            step = math.gcd(half, 256)
            parts = half // step
            for part in range(parts):
                order = INNER[len(chunks) % len(INNER)]
                chunks.append((index, part * step, step, out_index, column + part * step, order))
            column += half
    return chunks


class Place:
    def __init__(self, sizes):
        self.sizes = sizes
        self.me = lax.axis_index("dp")
        self.strides = [math.prod(sizes[i + 1 :]) for i in range(len(sizes))]
        self.coords = [
            lax.rem(lax.div(self.me, stride), size) for stride, size in zip(self.strides, sizes)
        ]
        self.base = [sum(size - 1 for size in sizes[:i]) for i in range(len(sizes))]

    def other(self, dim, offset):
        return lax.rem(self.coords[dim] + offset, self.sizes[dim])

    def peer(self, dim, offset):
        return self.me + (self.other(dim, offset) - self.coords[dim]) * self.strides[dim]

    def slot(self, dim, offset):
        return self.base[dim] + offset - 1

    def barrier(self, extra=()):
        barrier = pltpu.get_barrier_semaphore()
        count = 0
        for dim, size in enumerate(self.sizes):
            for offset in range(1, size):
                pl.semaphore_signal(
                    barrier, inc=1, device_id={"dp": self.peer(dim, offset)}, device_id_type=MESH
                )
                count += 1
        for target in extra:
            pl.semaphore_signal(barrier, inc=1, device_id=target, device_id_type=MESH)
            count += 1
        pl.semaphore_wait(barrier, count)


def remote(source, target, send, recv, device):
    return pltpu.make_async_remote_copy(
        src_ref=source,
        dst_ref=target,
        send_sem=send,
        recv_sem=recv,
        device_id=device,
        device_id_type=MESH,
    )


def gather_kernel(sizes, chunks, counts, *refs):
    n_in, n_out, n_rows = counts
    refs = list(refs)
    ins = [refs.pop(0) for _ in range(n_in)]
    row_ins = [refs.pop(0) for _ in range(n_rows)]
    length_in = refs.pop(0)
    outs = [refs.pop(0) for _ in range(n_out)]
    row_outs = [refs.pop(0) for _ in range(n_rows)]
    length_out = refs.pop(0)
    send_sem, recv_sem, local_sem, row_send, row_recv, length_sem = refs
    place = Place(sizes)
    k = len(sizes)
    mine = place.coords[PAIR]
    theirs = place.other(PAIR, 1)
    tensor_me = lax.axis_index("tensor")
    near = {"tensor": 1 - tensor_me}
    far = {"dp": place.peer(PAIR, 1)}

    def region(chunk, done, dim=None, coord=None):
        where = []
        for i in range(k):
            if i == dim:
                where.append(coord)
            elif i in done:
                where.append(slice(None))
            else:
                where.append(place.coords[i])
        return outs[chunk[3]].at[tuple(where) + (slice(None), pl.ds(chunk[4], chunk[2]))]

    def source_of(chunk, half_index):
        half = ins[chunk[0]].shape[1] // 2
        start = pl.multiple_of(half_index * half + chunk[1], 128)
        return ins[chunk[0]].at[:, pl.ds(start, chunk[2])]

    def steps(chunk):
        return (PAIR,) + chunk[5]

    def sends(j, stage):
        chunk = chunks[j]
        order = steps(chunk)
        dim, done = order[stage], order[:stage]
        block = region(chunk, done)
        source = source_of(chunk, theirs) if stage == 0 else block
        return [
            remote(
                source,
                block,
                send_sem.at[j, place.slot(dim, offset)],
                recv_sem.at[j, place.slot(dim, offset)],
                {"dp": place.peer(dim, offset)},
            )
            for offset in range(1, sizes[dim])
        ]

    def wait_arrivals(j, stage):
        chunk = chunks[j]
        order = steps(chunk)
        dim, done = order[stage], order[:stage]
        for offset in range(1, sizes[dim]):
            block = region(chunk, done, dim, place.other(dim, sizes[dim] - offset))
            remote(
                block,
                block,
                send_sem.at[j, place.slot(dim, offset)],
                recv_sem.at[j, place.slot(dim, offset)],
                {"dp": place.peer(dim, offset)},
            ).wait_recv()

    place.barrier([near])
    started, own = [], []
    crossing = remote(
        length_in, length_out.at[mine], length_sem.at[0], length_sem.at[1], far
    )
    crossing.start()
    rows_far, rows_near, passed = [], [], []

    def send_rows(i):
        slot = row_outs[i].at[mine, tensor_me]
        rows_far.append(remote(row_ins[i], slot, row_send.at[i, 0], row_recv.at[i, 0], far))
        rows_near.append(remote(row_ins[i], slot, row_send.at[i, 1], row_recv.at[i, 1], near))
        rows_far[-1].start()
        rows_near[-1].start()
        row_outs[i][mine, tensor_me] = row_ins[i][...]

    def pass_rows(i):
        rows_far[i].wait()
        slot = row_outs[i].at[theirs, tensor_me]
        passed.append(remote(slot, slot, row_send.at[i, 2], row_recv.at[i, 2], near))
        passed[-1].start()

    def begin(j):
        copies = sends(j, 0)
        for copy in copies:
            copy.start()
        started.extend(copies)
        copy = pltpu.make_async_copy(
            source_of(chunks[j], mine), region(chunks[j], ()), local_sem.at[j]
        )
        copy.start()
        own.append(copy)

    for j in range(min(AHEAD, len(chunks))):
        begin(j)
    length_out[mine] = length_in[...]
    total_steps = len(chunks) + DEPTH * (k - 1)
    for step in range(total_steps):
        if step + AHEAD < len(chunks):
            begin(step + AHEAD)
        for i in range(n_rows):
            if step == min(4 + 3 * i, total_steps - 1):
                send_rows(i)
        for stage in range(k, 0, -1):
            j = step - DEPTH * (stage - 1)
            if not 0 <= j < len(chunks):
                continue
            if stage == 1:
                own[j].wait()
            wait_arrivals(j, stage - 1)
            if stage < k:
                copies = sends(j, stage)
                for copy in copies:
                    copy.start()
                started += copies
        for i in range(n_rows):
            if step == min(12 + i, total_steps - 1):
                pass_rows(i)
    crossing.wait()
    for copy in rows_near + passed:
        copy.wait()
    for copy in started:
        copy.wait_send()


def gather_all(weights, layouts, rows, length_row, collective_id):
    sizes = split_dims(lax.axis_size("dp"))
    chunks = pieces(layouts)
    peers = sum(size - 1 for size in sizes)
    n_in, n_out, n_rows = len(weights), len(layouts), len(rows)
    depth = weights[0].shape[0]
    whole = pl.BlockSpec(memory_space=pltpu.VMEM)
    outs = pl.pallas_call(
        functools.partial(gather_kernel, sizes, chunks, (n_in, n_out, n_rows)),
        out_shape=[
            jax.ShapeDtypeStruct(sizes + (depth, sum(half for _, half in members)), jnp.bfloat16)
            for members in layouts
        ]
        + [jax.ShapeDtypeStruct((2, 2) + r.shape, r.dtype) for r in rows]
        + [jax.ShapeDtypeStruct((2,) + length_row.shape, length_row.dtype)],
        in_specs=[whole] * (n_in + n_rows + 1),
        out_specs=[pl.BlockSpec(memory_space=pl.ANY)] * n_out + [whole] * (n_rows + 1),
        scratch_shapes=[
            pltpu.SemaphoreType.DMA((len(chunks), peers)),
            pltpu.SemaphoreType.DMA((len(chunks), peers)),
            pltpu.SemaphoreType.DMA((len(chunks),)),
            pltpu.SemaphoreType.DMA((n_rows, 3)),
            pltpu.SemaphoreType.DMA((n_rows, 3)),
            pltpu.SemaphoreType.DMA((2,)),
        ],
        compiler_params=pltpu.CompilerParams(
            collective_id=collective_id, has_side_effects=True, vmem_limit_bytes=VMEM_LIMIT
        ),
    )(*weights, *rows, length_row)
    full = [out.reshape(-1, out.shape[-1]) for out in outs[:n_out]]
    row_sets = [out.reshape(-1, out.shape[-1]) for out in outs[n_out : n_out + n_rows]]
    return full, row_sets, outs[n_out + n_rows][:, 0, 0]


def reduce_kernel(sizes, chunks, counts, tensor_size, *refs):
    n_in, n_out = counts
    refs = list(refs)
    ins = [refs.pop(0) for _ in range(n_in)]
    gains = refs.pop(0)
    outs = [refs.pop(0) for _ in range(n_out)]
    gain_out = refs.pop(0)
    k = len(sizes)
    m = k - 1
    held = [[refs.pop(0) for _ in range(m - 1)] for _ in chunks]
    landed = [[refs.pop(0) for _ in range(m)] for _ in chunks]
    crossed = [refs.pop(0) for _ in chunks]
    gain_held = [refs.pop(0) for _ in range(k)]
    gain_landed = [refs.pop(0) for _ in range(k + 1)]
    send_sem, recv_sem, local_sem, gain_send, gain_recv = refs
    place = Place(sizes)
    tensor_me = lax.axis_index("tensor")
    mine = place.coords[PAIR]
    theirs = place.other(PAIR, 1)
    rows = ins[0].shape[-2]

    def order_of(j):
        return tuple(reversed(chunks[j][5]))

    def part(ref, dims, dim, coord, columns):
        where = tuple(coord if i == dim else slice(None) for i in dims)
        return ref.at[where + (slice(None), columns)]

    def copies_of(j, stage):
        _, _, width, array, column, _ = chunks[j]
        order = order_of(j)
        dim = order[stage]
        dims = [i for i in range(k) if i not in order[:stage]]
        if stage == 0:
            ref, columns = ins[array], pl.ds(column, width)
        else:
            ref, columns = held[j][stage - 1], slice(None)
        return [
            remote(
                part(ref, dims, dim, place.other(dim, offset), columns),
                landed[j][stage].at[offset - 1],
                send_sem.at[j, place.slot(dim, offset)],
                recv_sem.at[j, place.slot(dim, offset)],
                {"dp": place.peer(dim, offset)},
            )
            for offset in range(1, sizes[dim])
        ]

    def result_at(j):
        index, start, width = chunks[j][:3]
        half = outs[index].shape[1] // 2
        return outs[index], pl.ds(pl.multiple_of(mine * half + start, 128), width)

    def cross_copy(j):
        out, columns = result_at(j)
        slot = place.slot(PAIR, 1)
        return remote(
            crossed[j],
            out.at[:, columns],
            send_sem.at[j, slot],
            recv_sem.at[j, slot],
            {"dp": place.peer(PAIR, 1)},
        )

    def add_up(j, stage):
        order = order_of(j)
        dim = order[stage]
        dims = [i for i in range(k) if i not in order[:stage]]
        lead = [sizes[i] for i in dims if i != dim]
        per = rows // 16

        def total_of(where, rows_at):
            if stage == 0:
                own = tuple(where)
                source = held[j][0]
            else:
                own = list(where)
                own.insert(dims.index(dim), place.coords[dim])
                own = tuple(own)
                source = held[j][stage - 1]
            total = source[own + (rows_at, slice(None))].astype(jnp.float32)
            for offset in range(1, sizes[dim]):
                got = landed[j][stage][(offset - 1,) + tuple(where) + (rows_at, slice(None))]
                total = total + got.astype(jnp.float32)
            return total

        if stage == m - 1:

            def last(i, carry):
                rows_at = pl.ds(pl.multiple_of(i * 16, 16), 16)
                crossed[j][rows_at, :] = total_of((theirs,), rows_at)
                return carry

            lax.fori_loop(0, per, last, 0)
            copy = cross_copy(j)
            copy.start()

            def keep(i, carry):
                rows_at = pl.ds(pl.multiple_of(i * 16, 16), 16)
                out, columns = result_at(j)
                out[rows_at, columns] = total_of((mine,), rows_at)
                return carry

            lax.fori_loop(0, per, keep, 0)
            return copy

        def body(i, carry):
            rows_at = pl.ds(pl.multiple_of(lax.rem(i, per) * 16, 16), 16)
            flat = lax.div(i, per)
            where = []
            for position in range(len(lead)):
                below = math.prod(lead[position + 1 :])
                where.append(lax.rem(lax.div(flat, below), lead[position]))
            total = total_of(where, rows_at)
            held[j][stage][tuple(where) + (rows_at, slice(None))] = total.astype(jnp.bfloat16)
            return carry

        lax.fori_loop(0, math.prod(lead) * per, body, 0)
        return None

    def gain_copies(stage):
        source = gains if stage == 0 else gain_held[stage - 1]
        result = []
        if stage < k:
            for offset in range(1, sizes[stage]):
                slot = place.slot(stage, offset)
                result.append(
                    remote(
                        source,
                        gain_landed[stage].at[offset - 1],
                        gain_send.at[slot],
                        gain_recv.at[slot],
                        {"dp": place.peer(stage, offset)},
                    )
                )
        else:
            first = sum(size - 1 for size in sizes)
            for offset in range(1, tensor_size):
                result.append(
                    remote(
                        source,
                        gain_landed[stage].at[offset - 1],
                        gain_send.at[first + offset - 1],
                        gain_recv.at[first + offset - 1],
                        {"tensor": lax.rem(tensor_me + offset, tensor_size)},
                    )
                )
        return result

    place.barrier(
        [{"tensor": lax.rem(tensor_me + i, tensor_size)} for i in range(1, tensor_size)]
    )
    flights, own, crossing = [], [], []

    def begin(j):
        _, _, width, array, column, _ = chunks[j]
        first = copies_of(j, 0)
        for copy in first:
            copy.start()
        flights.append([first])
        dim = order_of(j)[0]
        copy = pltpu.make_async_copy(
            part(ins[array], range(k), dim, place.coords[dim], pl.ds(column, width)),
            held[j][0],
            local_sem.at[j],
        )
        copy.start()
        own.append(copy)

    for j in range(min(RUN, len(chunks))):
        begin(j)
    gain_flight = gain_copies(0)
    for copy in gain_flight:
        copy.start()
    for step in range(len(chunks) + LAG * (m - 1)):
        if step + RUN < len(chunks):
            begin(step + RUN)
        if step % 2 == 1 and step // 2 <= k:
            turn = step // 2
            for copy in gain_flight:
                copy.wait()
            total = (gains if turn == 0 else gain_held[turn - 1])[...]
            for i in range(len(gain_flight)):
                total = total + gain_landed[turn][i]
            if turn < k:
                gain_held[turn][...] = total
                gain_flight = gain_copies(turn + 1)
                for copy in gain_flight:
                    copy.start()
            else:
                gain_out[...] = total
        for stage in range(m - 1, -1, -1):
            j = step - LAG * stage
            if not 0 <= j < len(chunks):
                continue
            if stage == 0:
                own[j].wait()
            for copy in flights[j][stage]:
                copy.wait_recv()
            copy = add_up(j, stage)
            if stage < m - 1:
                following = copies_of(j, stage + 1)
                for copy in following:
                    copy.start()
                flights[j].append(following)
            else:
                crossing.append(copy)
    for copy in crossing:
        copy.wait_recv()
    for flight in flights:
        for copies in flight:
            for copy in copies:
                copy.wait_send()
    for copy in crossing:
        copy.wait_send()


def reduce_weights(grads, layouts, widths, gains, collective_id):
    sizes = split_dims(lax.axis_size("dp"))
    tensor_size = lax.axis_size("tensor")
    k = len(sizes)
    m = k - 1
    rows = grads[0].shape[0] // math.prod(sizes)
    chunks = pieces(layouts)
    peers = sum(size - 1 for size in sizes)
    n_in, n_out = len(grads), len(widths)
    held, landed, crossed = [], [], []
    for _, _, width, _, _, gather_order in chunks:
        order = tuple(reversed(gather_order))
        for stage in range(m):
            left = tuple(sizes[i] for i in range(k) if i not in order[: stage + 1])
            if stage < m - 1:
                held.append(pltpu.VMEM(left + (rows, width), jnp.bfloat16))
            landed.append(pltpu.VMEM((sizes[order[stage]] - 1,) + left + (rows, width), jnp.bfloat16))
        crossed.append(pltpu.VMEM((rows, width), jnp.float32))
    gain_landed = [pltpu.VMEM((size - 1,) + gains.shape, jnp.float32) for size in sizes + (tensor_size,)]
    whole = pl.BlockSpec(memory_space=pltpu.VMEM)
    outs = pl.pallas_call(
        functools.partial(reduce_kernel, sizes, chunks, (n_in, n_out), tensor_size),
        out_shape=[jax.ShapeDtypeStruct((rows, width), jnp.float32) for width in widths]
        + [jax.ShapeDtypeStruct(gains.shape, jnp.float32)],
        in_specs=[pl.BlockSpec(memory_space=pl.ANY)] * n_in + [whole],
        out_specs=[whole] * (n_out + 1),
        scratch_shapes=held
        + landed
        + crossed
        + [pltpu.VMEM(gains.shape, jnp.float32)] * k
        + gain_landed
        + [
            pltpu.SemaphoreType.DMA((len(chunks), peers)),
            pltpu.SemaphoreType.DMA((len(chunks), peers)),
            pltpu.SemaphoreType.DMA((len(chunks),)),
            pltpu.SemaphoreType.DMA((peers + tensor_size - 1,)),
            pltpu.SemaphoreType.DMA((peers + tensor_size - 1,)),
        ],
        compiler_params=pltpu.CompilerParams(
            collective_id=collective_id, has_side_effects=True, vmem_limit_bytes=VMEM_LIMIT
        ),
    )(*[g.reshape(sizes + (rows, g.shape[1])) for g in grads], gains)
    return outs[:n_out], outs[n_out]


def group_place():
    sizes = split_dims(lax.axis_size("dp"))
    place = Place(sizes)
    tensor_me = lax.axis_index("tensor")
    near = {"tensor": 1 - tensor_me}
    far = {"dp": place.peer(PAIR, 1)}
    return place.coords[PAIR], place.other(PAIR, 1), tensor_me, near, far


def group_barrier(near, far):
    barrier = pltpu.get_barrier_semaphore()
    pl.semaphore_signal(barrier, inc=1, device_id=near, device_id_type=MESH)
    pl.semaphore_signal(barrier, inc=1, device_id=far, device_id_type=MESH)
    pl.semaphore_wait(barrier, 2)


def gather_rows_kernel(in_ref, out_ref, send_sem, recv_sem):
    mine, theirs, tensor_me, near, far = group_place()
    group_barrier(near, far)
    rows = in_ref.shape[0] // PARTS
    across, beside, passed = [], [], []
    for i in range(PARTS):
        source = in_ref.at[pl.ds(i * rows, rows)]
        slot = out_ref.at[mine, tensor_me, pl.ds(i * rows, rows)]
        across.append(remote(source, slot, send_sem.at[0, i], recv_sem.at[0, i], far))
        beside.append(remote(source, slot, send_sem.at[1, i], recv_sem.at[1, i], near))
        across[-1].start()
        beside[-1].start()
    out_ref[mine, tensor_me] = in_ref[...]
    for i in range(PARTS):
        across[i].wait()
        slot = out_ref.at[theirs, tensor_me, pl.ds(i * rows, rows)]
        passed.append(remote(slot, slot, send_sem.at[2, i], recv_sem.at[2, i], near))
        passed[-1].start()
    for copy in beside + passed:
        copy.wait()


def gather_rows(values, collective_id):
    out = pl.pallas_call(
        gather_rows_kernel,
        out_shape=jax.ShapeDtypeStruct((2, 2) + values.shape, values.dtype),
        in_specs=[pl.BlockSpec(memory_space=pltpu.VMEM)],
        out_specs=pl.BlockSpec(memory_space=pltpu.VMEM),
        scratch_shapes=[pltpu.SemaphoreType.DMA((3, PARTS))] * 2,
        compiler_params=pltpu.CompilerParams(collective_id=collective_id, has_side_effects=True),
    )(values)
    return out.reshape(-1, values.shape[-1])


def scatter_rows_kernel(count, *refs):
    refs = list(refs)
    ins = [refs.pop(0) for _ in range(count)]
    outs = [refs.pop(0) for _ in range(count)]
    landed = [refs.pop(0) for _ in range(count)]
    sent = [refs.pop(0) for _ in range(count)]
    got = [refs.pop(0) for _ in range(count)]
    send_sem, recv_sem = refs
    mine, theirs, tensor_me, near, far = group_place()
    group_barrier(near, far)
    parts = PARTS
    rows = outs[0].shape[0] // parts
    first, second, across = [], [], []

    def span(part):
        return pl.ds(part * rows, rows)

    for i in range(count):
        for part in range(parts):
            copy = remote(
                ins[i].at[theirs, 1 - tensor_me, span(part)],
                landed[i].at[0, span(part)],
                send_sem.at[i, 0, part],
                recv_sem.at[i, 0, part],
                near,
            )
            copy.start()
            first.append(copy)
        copy = remote(
            ins[i].at[mine, 1 - tensor_me],
            landed[i].at[1],
            send_sem.at[i, 1, 0],
            recv_sem.at[i, 1, 0],
            near,
        )
        copy.start()
        second.append(copy)
    for i in range(count):
        for part in range(parts):
            first[i * parts + part].wait_recv()

            def body(r, carry):
                at = pl.ds(pl.multiple_of(part * rows + r * 16, 16), 16)
                total = ins[i][theirs, tensor_me, at, :] + landed[i][0, at, :]
                sent[i][at, :] = total.astype(jnp.bfloat16)
                return carry

            lax.fori_loop(0, rows // 16, body, 0)
            copy = remote(
                sent[i].at[span(part)],
                got[i].at[span(part)],
                send_sem.at[i, 2, part],
                recv_sem.at[i, 2, part],
                far,
            )
            copy.start()
            across.append(copy)
    for i in range(count):
        second[i].wait_recv()
        for part in range(parts):
            across[i * parts + part].wait_recv()

            def body(r, carry):
                at = pl.ds(pl.multiple_of(part * rows + r * 16, 16), 16)
                total = ins[i][mine, tensor_me, at, :] + landed[i][1, at, :]
                outs[i][at, :] = total + got[i][at, :].astype(jnp.float32)
                return carry

            lax.fori_loop(0, rows // 16, body, 0)
    for copy in first + second + across:
        copy.wait_send()


def scatter_rows(partials, collective_id):
    count = len(partials)
    rows, width = partials[0].shape[0] // 4, partials[0].shape[1]
    whole = pl.BlockSpec(memory_space=pltpu.VMEM)
    return pl.pallas_call(
        functools.partial(scatter_rows_kernel, count),
        out_shape=[jax.ShapeDtypeStruct((rows, width), jnp.float32)] * count,
        in_specs=[whole] * count,
        out_specs=[whole] * count,
        scratch_shapes=[pltpu.VMEM((2, rows, width), jnp.float32)] * count
        + [pltpu.VMEM((rows, width), jnp.bfloat16)] * (2 * count)
        + [pltpu.SemaphoreType.DMA((count, 3, PARTS))] * 2,
        compiler_params=pltpu.CompilerParams(
            collective_id=collective_id, has_side_effects=True, vmem_limit_bytes=VMEM_LIMIT
        ),
    )(*[p.reshape(2, 2, rows, width) for p in partials])


def turn(values, cosine, sine_part):
    return values * cosine + pltpu.roll(values, HEAD_SIZE // 2, 1) * sine_part


def dot_rows(left, right):
    return jnp.dot(left, right, preferred_element_type=jnp.float32)


def head_at(index):
    return slice(index * HEAD_SIZE, (index + 1) * HEAD_SIZE)


def attend_kernel(
    lengths, x, w, wo, gain_q, gain_k, cosine, sine_part,
    raw, rot, value, mixed, probs, out,
):
    length_rows = x.shape[0] // 2
    kv_heads = value.shape[1] // HEAD_SIZE
    ratio = mixed.shape[1] // value.shape[1]
    q_heads = kv_heads * ratio
    wide = 2 * HEAD_SIZE
    scaling = HEAD_SIZE ** (-0.5)
    row = lax.broadcasted_iota(jnp.int32, (length_rows, length_rows), 0)
    column = lax.broadcasted_iota(jnp.int32, (length_rows, length_rows), 1)
    for s in range(2):
        rows = slice(s * length_rows, (s + 1) * length_rows)
        x_rows = x[rows, :]
        for block in range(w.shape[1] // wide):
            at = slice(block * wide, (block + 1) * wide)
            projected = dot_rows(x_rows, w[:, at])
            if at.start < raw.shape[1]:
                raw[rows, at] = projected
            else:
                value[rows, at.start - raw.shape[1] : at.stop - raw.shape[1]] = projected.astype(
                    jnp.bfloat16
                )
        for head in range(q_heads + kv_heads):
            part = raw[rows, head_at(head)]
            gain = (gain_q if head < q_heads else gain_k)[...]
            normed, _ = rms_rows(part, gain)
            rot[rows, head_at(head)] = turn(normed, cosine[rows, :], sine_part[rows, :]).astype(
                jnp.bfloat16
            )
        live = (row < lengths[s]) & (column <= row)
        allowed = live | (row == column)
        for head in range(q_heads):
            group = head // ratio
            scores = product_t(rot[rows, head_at(head)], rot[rows, head_at(q_heads + group)])
            scores = jnp.where(allowed, scores * scaling, -1e30)
            row_max = jnp.max(scores, axis=-1, keepdims=True)
            total = jnp.sum(jnp.exp(scores - row_max), axis=-1, keepdims=True)
            shares = jnp.exp(scores - (row_max + jnp.log(total)))
            probs[s * q_heads + head] = shares
            mixed[rows, head_at(head)] = dot_rows(
                shares.astype(jnp.bfloat16), value[rows, head_at(group)]
            ).astype(jnp.bfloat16)
        for block in range(wo.shape[0] // wide):
            at = slice(block * wide, (block + 1) * wide)
            out[rows, at] = product_t(mixed[rows, :], wo[at, :])


def attend(lengths, normed, full_qkv, full_out, gain_query, gain_key, cosine, sine_part):
    rows = normed.shape[0]
    mixed_width = full_out.shape[1]
    value_width = (full_qkv.shape[1] - mixed_width) // 2
    raw_width = mixed_width + value_width
    count = 2 * (mixed_width // HEAD_SIZE)
    whole = pl.BlockSpec(memory_space=pltpu.VMEM)
    return pl.pallas_call(
        attend_kernel,
        out_shape=[
            jax.ShapeDtypeStruct((rows, raw_width), jnp.float32),
            jax.ShapeDtypeStruct((rows, raw_width), jnp.bfloat16),
            jax.ShapeDtypeStruct((rows, value_width), jnp.bfloat16),
            jax.ShapeDtypeStruct((rows, mixed_width), jnp.bfloat16),
            jax.ShapeDtypeStruct((count, rows // 2, rows // 2), jnp.float32),
            jax.ShapeDtypeStruct((rows, full_out.shape[0]), jnp.float32),
        ],
        in_specs=[pl.BlockSpec(memory_space=pltpu.SMEM)] + [whole] * 7,
        out_specs=[whole] * 6,
        compiler_params=pltpu.CompilerParams(vmem_limit_bytes=VMEM_LIMIT // 2),
    )(
        lengths, normed, full_qkv, full_out, gain_query[None], gain_key[None], cosine, sine_part
    )


def attend_back_kernel(
    grad, w, wo, gain_q, gain_k, cosine, sine_part, raw, rot, value, mixed, probs,
    grad_qkv, terms, gain_q_out, gain_k_out, grad_mixed,
):
    length_rows = grad.shape[0] // 2
    kv_heads = value.shape[1] // HEAD_SIZE
    ratio = mixed.shape[1] // value.shape[1]
    q_heads = kv_heads * ratio
    wide = 2 * HEAD_SIZE
    scaling = HEAD_SIZE ** (-0.5)
    gain_q_out[...] = jnp.zeros_like(gain_q_out)
    gain_k_out[...] = jnp.zeros_like(gain_k_out)
    for s in range(2):
        rows = slice(s * length_rows, (s + 1) * length_rows)

        def finish(grad_rot, head):
            gain, gain_out = (gain_q, gain_q_out) if head < q_heads else (gain_k, gain_k_out)
            upstream = turn(grad_rot, cosine[rows, :], -sine_part[rows, :])
            part = raw[rows, head_at(head)]
            _, inverse = rms_rows(part, gain[...])
            grad_raw, grad_gain = rms_back(upstream, part, inverse, gain[...])
            grad_qkv[rows, head_at(head)] = grad_raw.astype(jnp.bfloat16)
            gain_out[...] += grad_gain[None]

        grad_rows = grad[rows, :]
        for block in range(wo.shape[1] // wide):
            at = slice(block * wide, (block + 1) * wide)
            grad_mixed[:, at] = dot_rows(grad_rows, wo[:, at]).astype(jnp.bfloat16)
        for group in range(kv_heads):
            grad_key, grad_value = None, None
            for member in range(ratio):
                head = group * ratio + member
                shares = probs[s * q_heads + head]
                upstream = grad_mixed[:, head_at(head)]
                share_grads = product_t(upstream, value[rows, head_at(group)])
                delta = jnp.sum(
                    upstream.astype(jnp.float32)
                    * mixed[rows, head_at(head)].astype(jnp.float32),
                    axis=-1,
                    keepdims=True,
                )
                grad_scores = (shares * (share_grads - delta) * scaling).astype(jnp.bfloat16)
                to_value = product_tn(shares.astype(jnp.bfloat16), upstream)
                to_key = product_tn(grad_scores, rot[rows, head_at(head)])
                grad_value = to_value if grad_value is None else grad_value + to_value
                grad_key = to_key if grad_key is None else grad_key + to_key
                finish(dot_rows(grad_scores, rot[rows, head_at(q_heads + group)]), head)
            finish(grad_key, q_heads + group)
            grad_qkv[rows, head_at(q_heads + kv_heads + group)] = grad_value.astype(jnp.bfloat16)
        for block in range(w.shape[0] // wide):
            at = slice(block * wide, (block + 1) * wide)
            terms[rows, at] = product_t(grad_qkv[rows, :], w[at, :])


def attend_back(grad_attn, full_qkv, full_out, gain_query, gain_key, cosine, sine_part, saved):
    rows = grad_attn.shape[0]
    whole = pl.BlockSpec(memory_space=pltpu.VMEM)
    grad_qkv, terms, gain_q, gain_k = pl.pallas_call(
        attend_back_kernel,
        out_shape=[
            jax.ShapeDtypeStruct((rows, full_qkv.shape[1]), jnp.bfloat16),
            jax.ShapeDtypeStruct((rows, full_qkv.shape[0]), jnp.float32),
            jax.ShapeDtypeStruct((1, HEAD_SIZE), jnp.float32),
            jax.ShapeDtypeStruct((1, HEAD_SIZE), jnp.float32),
        ],
        in_specs=[whole] * 12,
        out_specs=[whole] * 4,
        scratch_shapes=[pltpu.VMEM((rows // 2, full_out.shape[1]), jnp.bfloat16)],
        compiler_params=pltpu.CompilerParams(vmem_limit_bytes=VMEM_LIMIT // 2),
    )(
        grad_attn, full_qkv, full_out, gain_query[None], gain_key[None], cosine, sine_part, *saved
    )
    return grad_qkv, terms, gain_q[0], gain_k[0]


def per_device(
    tokens,
    cotangent,
    lengths,
    w_query,
    key_matrix,
    value_matrix,
    w_out,
    w_gate,
    w_up,
    w_down,
    gain_attn,
    gain_mlp,
    gain_query,
    gain_key,
):
    own_rows = tokens.shape[0]
    total_rows = own_rows * 2
    weights = (w_query, key_matrix, value_matrix, w_out, w_gate, w_up, w_down)
    halves = [w.shape[1] // 2 for w in weights]
    layouts = (
        ((0, halves[0]), (1, halves[1]), (2, halves[2])),
        ((3, halves[3]),),
        ((4, halves[4]), (5, halves[5])),
        ((6, halves[6]),),
    )
    own_index = lax.axis_index("tensor") * own_rows + jnp.arange(own_rows, dtype=jnp.int32)
    own_live = own_index < lengths[0]
    cot_live = jnp.where(own_live[:, None], cotangent, jnp.zeros_like(cotangent))
    token_values = tokens.astype(jnp.float32)
    attn_norm, attn_inverse = rms_rows(token_values, gain_attn)
    length_row = jnp.broadcast_to(lengths.astype(jnp.float32)[:, None], (8, HEAD_SIZE))
    fetched, row_sets, length_pair = gather_all(
        weights, layouts, (attn_norm.astype(jnp.bfloat16), cot_live), length_row, 0
    )
    full_qkv, full_out, full_gu, full_down = fetched
    normed, grad_result = row_sets
    length_pair = length_pair.astype(jnp.int32)
    indices = jnp.arange(total_rows, dtype=jnp.int32)
    positions = jnp.where(indices[None] < length_pair[:, None], indices[None], 0).reshape(-1)
    cosine, sine_part = rope_tables(positions, HEAD_SIZE)
    cosine = jnp.concatenate([cosine, cosine], axis=1)
    sine_part = jnp.concatenate([-sine_part, sine_part], axis=1)
    qk_raw, rotated, value_part, mixed_flat, probs, mixed_terms = attend(
        length_pair, normed, full_qkv, full_out, gain_query, gain_key, cosine, sine_part
    )
    resid = token_values + scatter_rows([mixed_terms], 7)[0]
    mlp_norm, mlp_inverse = rms_rows(resid, gain_mlp)
    mlp_in = gather_rows(mlp_norm.astype(jnp.bfloat16), 4)
    gate_up = jnp.dot(mlp_in, full_gu, preferred_element_type=jnp.float32)
    gate_proj, up_proj = gate_up[:, : halves[4]], gate_up[:, halves[4] :]
    activation = (jax.nn.silu(gate_proj) * up_proj).astype(jnp.bfloat16)
    grad_act = jnp.dot(grad_result, full_down, preferred_element_type=jnp.float32)
    sigma = jax.nn.sigmoid(gate_proj)
    grad_gate = (grad_act * up_proj * sigma * (1.0 + gate_proj * (1.0 - sigma))).astype(
        jnp.bfloat16
    )
    grad_up = (grad_act * gate_proj * sigma).astype(jnp.bfloat16)
    grad_gu = jnp.concatenate([grad_gate, grad_up], axis=1)
    grad_mlp_in, down_rows = scatter_rows(
        [product_t(grad_gu, full_gu), product_t(activation, full_down)], 8
    )
    result = (resid + down_rows).astype(jnp.bfloat16)
    grad_w_down = product_tn(grad_result, activation)
    grad_w_gu = product_tn(mlp_in, grad_gu)
    grad_resid_mlp, grad_gain_mlp = rms_back(grad_mlp_in, resid, mlp_inverse, gain_mlp)
    grad_resid = cot_live.astype(jnp.float32) + grad_resid_mlp
    grad_attn = gather_rows(grad_resid.astype(jnp.bfloat16), 6)
    grad_w_out = product_tn(grad_attn, mixed_flat)
    saved = (qk_raw, rotated, value_part, mixed_flat, probs)
    grad_qkv, normed_terms, grad_gain_query, grad_gain_key = attend_back(
        grad_attn, full_qkv, full_out, gain_query, gain_key, cosine, sine_part, saved
    )
    grad_w_qkv = product_tn(normed, grad_qkv)
    grad_normed = scatter_rows([normed_terms], 10)[0]
    grad_tokens_attn, grad_gain_attn = rms_back(grad_normed, token_values, attn_inverse, gain_attn)
    grad_tokens = grad_resid + grad_tokens_attn
    gain_parts = (grad_gain_attn, grad_gain_mlp, grad_gain_query, grad_gain_key)
    gain_rows = [part.reshape(-1, HEAD_SIZE) for part in gain_parts]
    used = sum(part.shape[0] for part in gain_rows)
    gain_rows.append(jnp.zeros((-used % 8, HEAD_SIZE), jnp.float32))
    weight_sums, gain_sum = reduce_weights(
        [g.astype(jnp.bfloat16) for g in (grad_w_qkv, grad_w_out, grad_w_gu, grad_w_down)],
        layouts,
        [w.shape[1] for w in weights],
        jnp.concatenate(gain_rows, axis=0),
        collective_id=1,
    )
    gain_totals, row = [], 0
    for part in gain_parts:
        taken = part.shape[0] // HEAD_SIZE
        gain_totals.append(gain_sum[row : row + taken].reshape(-1))
        row += taken
    return (result, grad_tokens, *weight_sums, *gain_totals)


def solution(mesh):
    in_specs = (
        P(("dp", "tensor"), None),
        P(("dp", "tensor"), None),
        P("dp"),
        P("dp", "tensor"),
        P("dp", "tensor"),
        P("dp", "tensor"),
        P("dp", "tensor"),
        P("dp", "tensor"),
        P("dp", "tensor"),
        P("dp", "tensor"),
        P(),
        P(),
        P(),
        P(),
    )
    out_specs = (
        P(("dp", "tensor"), None),
        P(("dp", "tensor"), None),
        P("dp", "tensor"),
        P("dp", "tensor"),
        P("dp", "tensor"),
        P("dp", "tensor"),
        P("dp", "tensor"),
        P("dp", "tensor"),
        P("dp", "tensor"),
        P(),
        P(),
        P(),
        P(),
    )
    return jax.shard_map(
        per_device, mesh=mesh, in_specs=in_specs, out_specs=out_specs, check_vma=False
    )
```
